512 devices in a mesh: expert: 8 (over x_lo, y), shard: 64 (over x_hi, z, core).
Axes of the slice: x: 4 (x_hi: 2, x_lo: 2; x = x_hi * 2 + x_lo), y: 4, z: 16, core: 2. Of those that a mesh axis runs over, the one named last changes fastest.
Arguments:
- fast_weights: bfloat16 [8, 64, 1, 64, 14336], P('expert', 'shard'), may hold values from -0.25 to 0.25
- slow_weights: float32 [8, 1, 64, 14336], P('expert', None, None, 'shard'), may hold values from -0.09375 to 0.09375
- step_counts: int32 [8, 64], P('expert', 'shard'), may hold values from 1 to 16
- token_counts: int32 [8, 64], P('expert', 'shard'), may hold values from 100 to 897
Outputs:
- new_slow: float32 [8, 1, 64, 14336], P('expert', None, None, 'shard')
- reset_fast: bfloat16 [8, 1, 64, 14336], P('expert')
The draws below stay inside these ranges and needn't reach their ends.
All inputs are finite; a program needn't handle non-finite values.
Results may differ from the reference program's by a relative error of at most 0.001.
Values may be sent and summed in bfloat16 or wider, within the bound.
No kernel may reach another device: no remote copies, remote signals or barrier semaphores. Data moves between devices by JAX's collectives and lax.ppermute only.
A program may use at most 64 MiB of HBM per device.

```python
import jax
import jax.numpy as jnp
from jax import lax

D = 4096
FF = 14336
LAYERS = 1
ROWS = 64
EXPERTS = 8
REPLICAS = 64


def draw_token_counts(key, part):
    base = jax.random.randint(key, (EXPERTS, REPLICAS), 100, 300)
    replica = jnp.arange(REPLICAS, dtype=jnp.int32)[None, :]
    return (base * (REPLICAS - 1 + 2 * replica) // (REPLICAS - 1)).astype(jnp.int32)


def place_ends(array, key, smallest, largest):
    longest = array.shape.index(max(array.shape))
    spots = []
    for shift in (0, 1):
        where = [jax.random.randint(jax.random.fold_in(key, axis), (), 0, length) for axis, length in enumerate(array.shape)]
        where[longest] = (where[longest] + shift) % array.shape[longest]
        spots.append(tuple(where))
    return array.at[spots[0]].set(smallest).at[spots[1]].set(largest)


def spiked(entries, own_key, source, target, blocks, factor):
    def block_of(position):
        return (jnp.arange(entries.shape[position]) // (entries.shape[position] // blocks)).reshape((-1,) + (1,) * (entries.ndim - 1 - position))

    near = jax.random.permutation(own_key, blocks)[block_of(target)]
    other_side = (block_of(target) + blocks // 2) % blocks
    return jnp.where((block_of(source) == near) | (block_of(source) == other_side), factor * entries, entries)


def steps_of(key, dims, pieces, smallest, top_value):
    def one(axis_at, blocks):
        draws = jax.random.uniform(jax.random.fold_in(jax.random.fold_in(key, 6), axis_at), (blocks,), jnp.float32, smallest / len(pieces), top_value / len(pieces))
        return jnp.repeat(jnp.exp(draws), dims[axis_at] // blocks).reshape((-1,) + (1,) * (len(dims) - axis_at - 1))

    loudness = one(*pieces[0])
    for cut in pieces[1:]:
        loudness = loudness * one(*cut)
    return loudness


def bell_draw(stream_key, shape, width, reach, shards=(), held_as=jnp.bfloat16):
    loudness = steps_of(stream_key, shape, shards, -0.22, 0.18) if shards else 1.0
    result = jax.random.normal(stream_key, shape, jnp.float32) * width * loudness
    return jnp.minimum(jnp.maximum(result, -reach), reach).astype(held_as)


def heavy_noise(stream_key, extent, width, reach, cuts, heavy, held_as=jnp.bfloat16):
    drawn = width * jax.random.normal(stream_key, extent, jnp.float32)
    if cuts:
        drawn = drawn * steps_of(stream_key, extent, cuts, -0.22, 0.18)
    return jnp.clip(spiked(drawn, jax.random.fold_in(stream_key, 3), *heavy), -reach, reach).astype(held_as)


def setup_inputs(seed: int = 0) -> dict:
    keys = jax.random.split(jax.random.key(seed), 5)
    return {
        "fast_weights": heavy_noise(keys[0], (EXPERTS, REPLICAS, LAYERS, ROWS, FF), D ** -0.5, 0.25, ((0, 8), (1, 64)), (1, 4, 64, 4.0)),
        "slow_weights": bell_draw(keys[1], (EXPERTS, LAYERS, ROWS, FF), D ** -0.5, 0.09375, ((0, 8), (3, 64)), jnp.float32),
        "step_counts": place_ends(jax.random.randint(keys[2], (EXPERTS, REPLICAS), 1, 17), jax.random.fold_in(keys[2], 1), 1, 16).astype(jnp.int32),
        "token_counts": draw_token_counts(jax.random.fold_in(keys[4], 71), 0),
    }


outer_rate = 0.7


def mix_one(args):
    fast, share = args
    return jnp.einsum("r,rlmn->lmn", share, fast.astype(jnp.float32), precision=lax.Precision.HIGHEST)


def reference(fast_weights, slow_weights, step_counts, token_counts):
    tokens = token_counts.astype(jnp.float32)
    steps = step_counts.astype(jnp.float32)
    share = tokens / steps
    tok = jnp.sum(tokens, axis=1)
    work = jnp.sum(tokens * steps, axis=1)
    qsum = jnp.sum(share, axis=1)
    total = jnp.sum(tok)
    mixed = lax.map(mix_one, (fast_weights, share))
    rate = outer_rate * EXPERTS * work / (tok * total)
    rate = rate[:, None, None, None]
    qsum = qsum[:, None, None, None]
    new_slow = slow_weights + rate * (mixed - qsum * slow_weights)
    return new_slow, new_slow.astype(jnp.bfloat16)
```

```python
import jax
import jax.numpy as jnp
from jax import lax
from jax.experimental import pallas as pl
from jax.experimental.pallas import tpu as pltpu
from jax.sharding import Mesh
from jax.sharding import PartitionSpec as P

F32 = jnp.float32
BF16 = jnp.bfloat16

SHARD = ("x", "zh", "zl", "c")
NEAR = ("x", "zl", "c")

outer_rate = 0.7

ROWS = 64
OWN = 224
LANES = 128
REST = OWN - LANES
PIECE = ROWS * OWN // LANES
TOP = PIECE - ROWS
SLIVER = LANES - REST


def packed(block):
    rest = block[:, LANES:]
    tail = rest[TOP:]
    side = jnp.concatenate([tail[:, k * SLIVER : (k + 1) * SLIVER] for k in range(REST // SLIVER)], axis=0)
    return jnp.concatenate([block[:, :LANES], jnp.concatenate([rest[:TOP], side], axis=1)], axis=0)


def unpacked(piece):
    low = piece[ROWS:]
    side = low[:, REST:]
    n = ROWS - TOP
    tail = jnp.concatenate([side[k * n : (k + 1) * n] for k in range(REST // SLIVER)], axis=1)
    return jnp.concatenate([piece[:ROWS], jnp.concatenate([low[:, :REST], tail], axis=0)], axis=1)


NEAR_NOTES = 16
FAR_NOTES = 8


def as_bytes(count):
    high = count // 256
    return high.astype(F32), (count - 256 * high).astype(F32)


def sort_kernel(tokens, steps, group, fast, out):
    for k in range(out.shape[1]):
        for zh in range(fast.shape[1] // OWN // out.shape[1]):
            at = (zh * out.shape[1] + k) * OWN
            out[0, k, zh * PIECE : (zh + 1) * PIECE] = packed(fast[:, at : at + OWN])
    row = lax.broadcasted_iota(jnp.int32, (NEAR_NOTES, LANES), 0)
    notes = jnp.zeros((NEAR_NOTES, LANES), F32)
    for k, value in enumerate((*as_bytes(tokens[0, 0]), *as_bytes(steps[0, 0]), *as_bytes(group[0, 0]))):
        notes = jnp.where(row == k, value, notes)
    for k in range(out.shape[1]):
        out[0, k, out.shape[2] - NEAR_NOTES :] = notes.astype(BF16)


def near_sum_kernel(got, out):
    n, rows = got.shape[0], got.shape[1] - NEAR_NOTES
    notes = [got[s, rows:].astype(F32) for s in range(n)]
    counts = [[256 * v[2 * k : 2 * k + 1] + v[2 * k + 1 : 2 * k + 2] for k in range(3)] for v in notes]
    shares = [tokens / steps for tokens, steps, _ in counts]
    for zh in range(out.shape[0]):
        piece = slice(zh * PIECE, (zh + 1) * PIECE)
        total = shares[0] * got[0, piece].astype(F32)
        for s in range(1, n):
            total = total + shares[s] * got[s, piece].astype(F32)
        out[zh, :PIECE] = total
    row = lax.broadcasted_iota(jnp.int32, (FAR_NOTES, LANES), 0)
    sums = (
        sum(tokens for tokens, _, _ in counts),
        sum(tokens * steps for tokens, steps, _ in counts),
        sum(shares),
        sum(group for _, _, group in counts),
    )
    far = jnp.zeros((FAR_NOTES, LANES), F32)
    for k, value in enumerate(sums):
        far = jnp.where(row == k, value, far)
    for zh in range(out.shape[0]):
        out[zh, PIECE:] = far


def refresh_kernel(groups, got, slow, new_slow, copies):
    total = got[0]
    for s in range(1, got.shape[0]):
        total = total + got[s]
    notes = total[PIECE:]
    tok, work, qsum, everywhere = (notes[k : k + 1] for k in range(4))
    rate = outer_rate * groups * work / (tok * everywhere)
    mine = packed(slow[0, 0])
    fresh = mine + rate * (total[:PIECE] - qsum * mine)
    new_slow[0, 0] = unpacked(fresh)
    for k in range(copies.shape[0]):
        copies[k] = fresh.astype(BF16)


def lay_out_kernel(core, own, other, out):
    first = core[0, 0] == 0
    for zh in range(own.shape[2]):
        for zl in range(own.shape[1]):
            a, b = own[0, zl, zh].astype(F32), other[0, zl, zh].astype(F32)
            at = (zh * own.shape[1] + zl) * 2 * OWN
            out[:, at : at + OWN] = unpacked(jnp.where(first, a, b)).astype(BF16)
            out[:, at + OWN : at + 2 * OWN] = unpacked(jnp.where(first, b, a)).astype(BF16)


def call(kernel, out_shape, **more):
    return pl.pallas_call(
        kernel,
        out_shape=out_shape,
        compiler_params=pltpu.CompilerParams(vmem_limit_bytes=48 * 2**20),
        **more,
    )


def struct(shape, dtype):
    return jax.ShapeDtypeStruct(shape, dtype)


def swap(pieces, axis):
    return lax.all_to_all(pieces, axis, split_axis=0, concat_axis=0, tiled=True)


def shards(fast_weights, slow_weights, step_counts, token_counts):
    size = {a: lax.axis_size(a) for a in SHARD}
    groups = lax.axis_size("expert")
    near = size["x"] * size["zl"] * size["c"]
    quad = size["zl"] * size["c"]
    scalar = pl.BlockSpec(memory_space=pltpu.SMEM)

    spread = jnp.broadcast_to(token_counts[None], (groups, 1, 1))
    group = swap(spread, "expert").sum(axis=0)

    fast = fast_weights[0, 0, 0]
    rows = size["zh"] * PIECE + NEAR_NOTES
    half = fast.shape[1] // size["x"]
    sorted_pieces = call(
        sort_kernel,
        struct((size["x"], quad, rows, LANES), BF16),
        grid=(size["x"],),
        in_specs=[scalar, scalar, scalar, pl.BlockSpec((ROWS, half), lambda x: (0, x))],
        out_specs=pl.BlockSpec((1, quad, rows, LANES), lambda x: (x, 0, 0, 0)),
    )(token_counts, step_counts, group, fast)
    got = swap(sorted_pieces.reshape(near, rows, LANES), NEAR)
    partial = call(near_sum_kernel, struct((size["zh"], PIECE + FAR_NOTES, LANES), F32))(got)
    got = swap(partial, "zh")
    new_slow, copies = call(
        lambda *refs: refresh_kernel(groups, *refs),
        (struct(slow_weights.shape, F32), struct((size["zh"], PIECE, LANES), BF16)),
    )(got, slow_weights)
    column = swap(copies, "zh")
    plane = size["x"] * size["zl"]
    own = swap(jnp.broadcast_to(column[None], (plane, *column.shape)), ("x", "zl"))
    other = lax.ppermute(own, "c", [(0, 1), (1, 0)])
    shape = (size["x"], size["zl"], size["zh"], PIECE, LANES)
    block = pl.BlockSpec((1, *shape[1:]), lambda x: (x, 0, 0, 0, 0))
    reset = call(
        lay_out_kernel,
        struct(fast.shape, BF16),
        grid=(size["x"],),
        in_specs=[scalar, block, block],
        out_specs=pl.BlockSpec((ROWS, half), lambda x: (0, x)),
    )(lax.axis_index("c").astype(jnp.int32).reshape(1, 1), own.reshape(shape), other.reshape(shape))
    return new_slow, reset[None, None]


def solution(mesh):
    torus = Mesh(
        mesh.devices.reshape(mesh.shape["expert"], 2, 8, 2, 2),
        ("expert", *SHARD),
    )
    placed = (
        P("expert", SHARD, None, None, None),
        P("expert", None, None, SHARD),
        P("expert", SHARD),
        P("expert", SHARD),
    )
    return jax.shard_map(
        shards,
        mesh=torus,
        in_specs=placed,
        out_specs=(P("expert", None, None, SHARD), P("expert", None, None, None)),
        check_vma=False,
    )
```

```python
import jax
import jax.numpy as jnp
from jax import lax
from jax.experimental import pallas as pl
from jax.experimental.pallas import tpu as pltpu
from jax.sharding import Mesh
from jax.sharding import PartitionSpec as P

F32 = jnp.float32
BF16 = jnp.bfloat16

SHARD = ("x", "zh", "zl", "c")
NEAR = ("x", "zl", "c")

outer_rate = 0.7

ROWS = 64
OWN = 224
LANES = 128
QUAD = 4
WIDE = QUAD * OWN
STEP = 32
TAIL = 16
REST = ROWS - TAIL

PIECE = ROWS + REST

NEAR_NOTES = 16
FAR_NOTES = 8


def lane_group(shape):
    return lax.broadcasted_iota(jnp.int32, shape, 1) // STEP


def rolled(v, by):
    by %= LANES
    return jnp.concatenate([v[:, LANES - by :], v[:, : LANES - by]], axis=1) if by else v


def folded(res, k):
    free = QUAD - 1 - k
    tail = res[REST:]
    group = lane_group((TAIL, LANES))
    return jnp.concatenate(
        [jnp.where(group == free, rolled(tail, STEP * (m + 1)), res[m * TAIL : (m + 1) * TAIL]) for m in range(QUAD - 1)],
        axis=0,
    )


def unfolded(piece, k):
    free = QUAD - 1 - k
    group = lane_group((TAIL, LANES))
    tail = rolled(piece[:TAIL], -STEP)
    for m in range(1, QUAD - 1):
        moved = rolled(piece[m * TAIL : (m + 1) * TAIL], -STEP * (m + 1))
        tail = jnp.where(group == (free - m - 1) % QUAD, moved, tail)
    return jnp.concatenate([piece, tail], axis=0)


def own_parts(block, k):
    at = STEP * k
    res = [block[:, at + LANES :], jnp.zeros((ROWS, STEP), block.dtype), block[:, :at]]
    return block[:, at : at + LANES], folded(jnp.concatenate([r for r in res if r.shape[1]], axis=1), k)


def own_block(tile, piece, k):
    at = STEP * k
    res = unfolded(piece, k)
    parts = [res[:, LANES - at :] if k else res[:, :0], tile, res[:, : LANES - STEP - at]]
    return jnp.concatenate([p for p in parts if p.shape[1]], axis=1)


def as_bytes(count):
    high = count // 256
    return high.astype(F32), (count - 256 * high).astype(F32)


def sort_kernel(fast, out):
    group = lane_group((ROWS, LANES))
    for zh in range(fast.shape[1] // WIDE):
        lanes = [slice(zh * WIDE + i * LANES, zh * WIDE + (i + 1) * LANES) for i in range(2 * QUAD - 1)]
        odd = [fast[:, at].astype(F32) for at in lanes[1::2]]
        for k in range(QUAD):
            if k == 0:
                res = odd[0]
            elif k == QUAD - 1:
                res = odd[-1]
            else:
                res = jnp.where(group >= QUAD - k, odd[k - 1], odd[k])
            at = zh * PIECE
            out[0, k, at : at + ROWS] = fast[:, lanes[2 * k]]
            out[0, k, at + ROWS : at + PIECE] = folded(res, k).astype(BF16)


def notes_kernel(tokens, steps, experts, _, out):
    row = lax.broadcasted_iota(jnp.int32, (NEAR_NOTES, LANES), 0)
    notes = jnp.zeros((NEAR_NOTES, LANES), F32)
    for i, count in enumerate((tokens[0, 0], steps[0, 0], sum(experts[e, 0] for e in range(experts.shape[0])))):
        for j, value in enumerate(as_bytes(count)):
            notes = jnp.where(row == 2 * i + j, value, notes)
    for k in range(out.shape[1]):
        out[0, k] = notes.astype(BF16)


def near_sum_kernel(got, out):
    n, rows = got.shape[0], got.shape[1] - NEAR_NOTES
    notes = [got[s, rows:].astype(F32) for s in range(n)]
    counts = [[256 * v[2 * i : 2 * i + 1] + v[2 * i + 1 : 2 * i + 2] for i in range(3)] for v in notes]
    shares = [tokens / steps for tokens, steps, _ in counts]
    tok = sum(tokens for tokens, _, _ in counts)
    work = sum(tokens * steps for tokens, steps, _ in counts)
    everywhere = sum(group for _, _, group in counts)
    row = lax.broadcasted_iota(jnp.int32, (FAR_NOTES, LANES), 0)
    far = jnp.zeros((FAR_NOTES, LANES), F32)
    for i, value in enumerate((tok, work, sum(shares), everywhere)):
        far = jnp.where(row == i, value, far)
    for zh in range(out.shape[0]):
        piece = slice(zh * PIECE, (zh + 1) * PIECE)
        total = shares[0] * got[0, piece].astype(F32)
        for s in range(1, n):
            total = total + shares[s] * got[s, piece].astype(F32)
        out[zh, :PIECE] = total
        out[zh, PIECE:] = far


def refresh_kernel(groups, place, got, slow, new_slow, copies):
    total = got[0]
    for s in range(1, got.shape[0]):
        total = total + got[s]
    tok, work, qsum, everywhere = (total[PIECE + i : PIECE + i + 1] for i in range(4))
    rate = outer_rate * groups * work / (tok * everywhere)
    for k in range(QUAD):

        @pl.when(place[0, 0] == k)
        def _(k=k):
            mine = own_parts(slow[0, 0], k)
            tile = mine[0] + rate * (total[:ROWS] - qsum * mine[0])
            rest = mine[1] + rate * (total[ROWS:PIECE] - qsum * mine[1])
            new_slow[0, 0] = own_block(tile, rest, k)
            for i in range(copies.shape[0]):
                copies[i, :ROWS] = tile.astype(BF16)
                copies[i, ROWS:] = rest.astype(BF16)


def lay_out_kernel(core, own, other, out):
    def body(pieces):
        group = lane_group((ROWS, LANES))
        for zh in range(own.shape[2]):
            at = zh * WIDE
            for k in range(QUAD):
                out[:, at + 2 * k * LANES : at + (2 * k + 1) * LANES] = pieces[k % 2][0, k // 2, zh, :ROWS]
            res = [unfolded(pieces[k % 2][0, k // 2, zh, ROWS:].astype(F32), k) for k in range(QUAD)]
            for k in range(QUAD - 1):
                odd = jnp.where(group < QUAD - 1 - k, res[k], res[k + 1])
                out[:, at + (2 * k + 1) * LANES : at + (2 * k + 2) * LANES] = odd.astype(BF16)

    @pl.when(core[0, 0] == 0)
    def _():
        body((own, other))

    @pl.when(core[0, 0] != 0)
    def _():
        body((other, own))


def call(kernel, out_shape, **more):
    return pl.pallas_call(
        kernel,
        out_shape=out_shape,
        compiler_params=pltpu.CompilerParams(vmem_limit_bytes=48 * 2**20),
        **more,
    )


def struct(shape, dtype):
    return jax.ShapeDtypeStruct(shape, dtype)


def swap(pieces, axis):
    return lax.all_to_all(pieces, axis, split_axis=0, concat_axis=0, tiled=True)


SCALAR = pl.BlockSpec(memory_space=pltpu.SMEM)
WHOLE = pl.BlockSpec(memory_space=pltpu.VMEM)


def scalar(value):
    return value.astype(jnp.int32).reshape(1, 1)


def shards(fast_weights, slow_weights, step_counts, token_counts):
    size = {a: lax.axis_size(a) for a in SHARD}
    groups = lax.axis_size("expert")
    nx, nzh, near = size["x"], size["zh"], size["x"] * size["zl"] * size["c"]
    core = lax.axis_index("c")
    place = scalar(lax.axis_index("zl") * size["c"] + core)
    core = scalar(core)

    fast = fast_weights[0, 0, 0]
    half = fast.shape[1] // nx
    halves = pl.BlockSpec((ROWS, half), lambda x: (0, x))

    def by_x(*shape):
        return pl.BlockSpec((1, *shape[1:]), lambda x: (x, *(0 for _ in shape[1:])))

    experts = swap(jnp.broadcast_to(token_counts, (groups, 1)), "expert")
    shape = (nx, QUAD, nzh * PIECE + NEAR_NOTES, LANES)
    pieces = call(sort_kernel, struct(shape, BF16), grid=(nx,), in_specs=[halves], out_specs=by_x(*shape))(fast)
    pieces = call(
        notes_kernel,
        struct(shape, BF16),
        grid=(nx,),
        in_specs=[SCALAR, SCALAR, SCALAR, pl.BlockSpec(memory_space=pl.ANY)],
        out_specs=pl.BlockSpec((1, QUAD, NEAR_NOTES, LANES), lambda x: (x, 0, shape[2] // NEAR_NOTES - 1, 0)),
        input_output_aliases={3: 0},
    )(token_counts, step_counts, experts, pieces)
    got = swap(pieces.reshape(near, *shape[2:]), NEAR)
    coded = call(near_sum_kernel, struct((nzh, PIECE + FAR_NOTES, LANES), F32))(got)
    got = swap(coded, "zh")
    new_slow, copies = call(
        lambda *refs: refresh_kernel(groups, *refs),
        (struct(slow_weights.shape, F32), struct((nzh, PIECE, LANES), BF16)),
        in_specs=[SCALAR, WHOLE, WHOLE],
    )(place, got, slow_weights)

    column = swap(copies, "zh")
    plane = nx * size["zl"]
    own = swap(jnp.broadcast_to(column[None], (plane, *column.shape)), ("x", "zl"))
    other = lax.ppermute(own, "c", [(0, 1), (1, 0)])
    shape = (nx, size["zl"], *column.shape)
    reset = call(
        lay_out_kernel,
        struct(fast.shape, BF16),
        grid=(nx,),
        in_specs=[SCALAR, by_x(*shape), by_x(*shape)],
        out_specs=halves,
    )(core, own.reshape(shape), other.reshape(shape))
    return new_slow, reset[None, None]


def solution(mesh):
    torus = Mesh(
        mesh.devices.reshape(mesh.shape["expert"], 2, 8, 2, 2),
        ("expert", *SHARD),
    )
    placed = (
        P("expert", SHARD, None, None, None),
        P("expert", None, None, SHARD),
        P("expert", SHARD),
        P("expert", SHARD),
    )
    return jax.shard_map(
        shards,
        mesh=torus,
        in_specs=placed,
        out_specs=(P("expert", None, None, SHARD), P("expert", None, None, None)),
        check_vma=False,
    )
```

```python
import jax
import jax.numpy as jnp
from jax import lax
from jax.experimental import pallas as pl
from jax.experimental.pallas import tpu as pltpu
from jax.sharding import Mesh
from jax.sharding import PartitionSpec as P

F32 = jnp.float32
BF16 = jnp.bfloat16

SHARD = ("x", "zh", "zl", "c")
NEAR = ("x", "zl", "c")

outer_rate = 0.7

ROWS = 64
OWN = 224
LANES = 128
QUAD = 4
WIDE = QUAD * OWN
STEP = 32
TAIL = 16
REST = ROWS - TAIL

PIECE = ROWS + REST

NEAR_NOTES = 16
FAR_NOTES = 8
TOP = 32767.0
DIGIT = 4096.0
MIDDLE = 32768.0
FINE = 8.0


def lane_group(shape):
    return lax.broadcasted_iota(jnp.int32, shape, 1) // STEP


def rolled(v, by):
    by %= LANES
    return jnp.concatenate([v[:, LANES - by :], v[:, : LANES - by]], axis=1) if by else v


def folded(res, k):
    free = QUAD - 1 - k
    tail = res[REST:]
    group = lane_group((TAIL, LANES))
    return jnp.concatenate(
        [jnp.where(group == free, rolled(tail, STEP * (m + 1)), res[m * TAIL : (m + 1) * TAIL]) for m in range(QUAD - 1)],
        axis=0,
    )


def unfolded(piece, k):
    free = QUAD - 1 - k
    group = lane_group((TAIL, LANES))
    tail = rolled(piece[:TAIL], -STEP)
    for m in range(1, QUAD - 1):
        moved = rolled(piece[m * TAIL : (m + 1) * TAIL], -STEP * (m + 1))
        tail = jnp.where(group == (free - m - 1) % QUAD, moved, tail)
    return jnp.concatenate([piece, tail], axis=0)


def own_parts(block, k):
    at = STEP * k
    res = [block[:, at + LANES :], jnp.zeros((ROWS, STEP), block.dtype), block[:, :at]]
    return block[:, at : at + LANES], folded(jnp.concatenate([r for r in res if r.shape[1]], axis=1), k)


def own_block(tile, piece, k):
    at = STEP * k
    res = unfolded(piece, k)
    parts = [res[:, LANES - at :] if k else res[:, :0], tile, res[:, : LANES - STEP - at]]
    return jnp.concatenate([p for p in parts if p.shape[1]], axis=1)


def as_bytes(count):
    high = count // 256
    return high.astype(F32), (count - 256 * high).astype(F32)


def sort_kernel(fast, out):
    group = lane_group((ROWS, LANES))
    for zh in range(fast.shape[1] // WIDE):
        lanes = [slice(zh * WIDE + i * LANES, zh * WIDE + (i + 1) * LANES) for i in range(2 * QUAD - 1)]
        odd = [fast[:, at].astype(F32) for at in lanes[1::2]]
        for k in range(QUAD):
            if k == 0:
                res = odd[0]
            elif k == QUAD - 1:
                res = odd[-1]
            else:
                res = jnp.where(group >= QUAD - k, odd[k - 1], odd[k])
            at = zh * PIECE
            out[0, k, at : at + ROWS] = fast[:, lanes[2 * k]]
            out[0, k, at + ROWS : at + PIECE] = folded(res, k).astype(BF16)


def notes_kernel(tokens, steps, experts, _, out):
    row = lax.broadcasted_iota(jnp.int32, (NEAR_NOTES, LANES), 0)
    notes = jnp.zeros((NEAR_NOTES, LANES), F32)
    for i, count in enumerate((tokens[0, 0], steps[0, 0], sum(experts[e, 0] for e in range(experts.shape[0])))):
        for j, value in enumerate(as_bytes(count)):
            notes = jnp.where(row == 2 * i + j, value, notes)
    for k in range(out.shape[1]):
        out[0, k] = notes.astype(BF16)


def near_sum_kernel(got, out):
    n, rows = got.shape[0], got.shape[1] - NEAR_NOTES
    notes = [got[s, rows:].astype(F32) for s in range(n)]
    counts = [[256 * v[2 * i : 2 * i + 1] + v[2 * i + 1 : 2 * i + 2] for i in range(3)] for v in notes]
    shares = [tokens / steps for tokens, steps, _ in counts]
    tok = sum(tokens for tokens, _, _ in counts)
    work = sum(tokens * steps for tokens, steps, _ in counts)
    everywhere = sum(group for _, _, group in counts)
    qsum = sum(shares)
    whole = jnp.floor(qsum)
    part = (qsum - whole) * DIGIT
    digit = jnp.floor(part)
    high = jnp.floor(work / DIGIT)
    fixed = (tok, high, work - DIGIT * high, everywhere - MIDDLE, whole, digit, jnp.floor((part - digit) * DIGIT))
    row = lax.broadcasted_iota(jnp.int32, (FAR_NOTES, LANES), 0)
    far = jnp.zeros((FAR_NOTES, LANES), F32)
    for i, value in enumerate(fixed):
        far = jnp.where(row == i + 1, value, far)
    for zh in range(out.shape[0]):
        piece = slice(zh * PIECE, (zh + 1) * PIECE)
        total = shares[0] * got[0, piece].astype(F32)
        for s in range(1, n):
            total = total + shares[s] * got[s, piece].astype(F32)
        largest = jnp.maximum(jnp.max(jnp.abs(total), axis=0, keepdims=True), 1e-30)
        level = jnp.ceil(FINE * jnp.log2(largest))
        coded = jnp.clip(jnp.round(total * (TOP * jnp.exp2(level * (-1 / FINE)))), -TOP, TOP)
        out[zh, :PIECE] = coded.astype(jnp.int32).astype(jnp.int16)
        out[zh, PIECE:] = jnp.where(row == 0, level, far).astype(jnp.int32).astype(jnp.int16)


def refresh_kernel(groups, place, got, slow, new_slow, copies):
    total = sums = None
    for s in range(got.shape[0]):
        notes = got[s, PIECE:].astype(jnp.int32).astype(F32)
        unit = jnp.exp2(notes[0:1] * (1 / FINE)) * (1 / TOP)
        part = unit * got[s, :PIECE].astype(jnp.int32).astype(F32)
        total, sums = (part, notes) if s == 0 else (total + part, sums + notes)
    tok = sums[1:2]
    work = DIGIT * sums[2:3] + sums[3:4]
    everywhere = sums[4:5] + MIDDLE * got.shape[0]
    qsum = sums[5:6] + (sums[6:7] + sums[7:8] * (1 / DIGIT)) * (1 / DIGIT)
    rate = outer_rate * groups * work / (tok * everywhere)
    for k in range(QUAD):

        @pl.when(place[0, 0] == k)
        def _(k=k):
            mine = own_parts(slow[0, 0], k)
            tile = mine[0] + rate * (total[:ROWS] - qsum * mine[0])
            rest = mine[1] + rate * (total[ROWS:] - qsum * mine[1])
            new_slow[0, 0] = own_block(tile, rest, k)
            for i in range(copies.shape[0]):
                copies[i, :ROWS] = tile.astype(BF16)
                copies[i, ROWS:] = rest.astype(BF16)


def lay_out_kernel(core, own, other, out):
    def body(pieces):
        group = lane_group((ROWS, LANES))
        for zh in range(own.shape[2]):
            at = zh * WIDE
            for k in range(QUAD):
                out[:, at + 2 * k * LANES : at + (2 * k + 1) * LANES] = pieces[k % 2][0, k // 2, zh, :ROWS]
            res = [unfolded(pieces[k % 2][0, k // 2, zh, ROWS:].astype(F32), k) for k in range(QUAD)]
            for k in range(QUAD - 1):
                odd = jnp.where(group < QUAD - 1 - k, res[k], res[k + 1])
                out[:, at + (2 * k + 1) * LANES : at + (2 * k + 2) * LANES] = odd.astype(BF16)

    @pl.when(core[0, 0] == 0)
    def _():
        body((own, other))

    @pl.when(core[0, 0] != 0)
    def _():
        body((other, own))


def call(kernel, out_shape, **more):
    return pl.pallas_call(
        kernel,
        out_shape=out_shape,
        compiler_params=pltpu.CompilerParams(vmem_limit_bytes=48 * 2**20),
        **more,
    )


def struct(shape, dtype):
    return jax.ShapeDtypeStruct(shape, dtype)


def swap(pieces, axis):
    return lax.all_to_all(pieces, axis, split_axis=0, concat_axis=0, tiled=True)


SCALAR = pl.BlockSpec(memory_space=pltpu.SMEM)
WHOLE = pl.BlockSpec(memory_space=pltpu.VMEM)


def scalar(value):
    return value.astype(jnp.int32).reshape(1, 1)


def shards(fast_weights, slow_weights, step_counts, token_counts):
    size = {a: lax.axis_size(a) for a in SHARD}
    groups = lax.axis_size("expert")
    nx, nzh, near = size["x"], size["zh"], size["x"] * size["zl"] * size["c"]
    core = lax.axis_index("c")
    place = scalar(lax.axis_index("zl") * size["c"] + core)
    core = scalar(core)

    fast = fast_weights[0, 0, 0]
    half = fast.shape[1] // nx
    halves = pl.BlockSpec((ROWS, half), lambda x: (0, x))

    def by_x(*shape):
        return pl.BlockSpec((1, *shape[1:]), lambda x: (x, *(0 for _ in shape[1:])))

    experts = swap(jnp.broadcast_to(token_counts, (groups, 1)), "expert")
    shape = (nx, QUAD, nzh * PIECE + NEAR_NOTES, LANES)
    pieces = call(sort_kernel, struct(shape, BF16), grid=(nx,), in_specs=[halves], out_specs=by_x(*shape))(fast)
    pieces = call(
        notes_kernel,
        struct(shape, BF16),
        grid=(nx,),
        in_specs=[SCALAR, SCALAR, SCALAR, pl.BlockSpec(memory_space=pl.ANY)],
        out_specs=pl.BlockSpec((1, QUAD, NEAR_NOTES, LANES), lambda x: (x, 0, shape[2] // NEAR_NOTES - 1, 0)),
        input_output_aliases={3: 0},
    )(token_counts, step_counts, experts, pieces)
    got = swap(pieces.reshape(near, *shape[2:]), NEAR)
    coded = call(near_sum_kernel, struct((nzh, PIECE + FAR_NOTES, LANES), jnp.int16))(got)
    got = swap(coded, "zh")
    new_slow, copies = call(
        lambda *refs: refresh_kernel(groups, *refs),
        (struct(slow_weights.shape, F32), struct((nzh, PIECE, LANES), BF16)),
        in_specs=[SCALAR, WHOLE, WHOLE],
    )(place, got, slow_weights)

    column = swap(copies, "zh")
    plane = nx * size["zl"]
    own = swap(jnp.broadcast_to(column[None], (plane, *column.shape)), ("x", "zl"))
    other = lax.ppermute(own, "c", [(0, 1), (1, 0)])
    shape = (nx, size["zl"], *column.shape)
    reset = call(
        lay_out_kernel,
        struct(fast.shape, BF16),
        grid=(nx,),
        in_specs=[SCALAR, by_x(*shape), by_x(*shape)],
        out_specs=halves,
    )(core, own.reshape(shape), other.reshape(shape))
    return new_slow, reset[None, None]


def solution(mesh):
    torus = Mesh(
        mesh.devices.reshape(mesh.shape["expert"], 2, 8, 2, 2),
        ("expert", *SHARD),
    )
    placed = (
        P("expert", SHARD, None, None, None),
        P("expert", None, None, SHARD),
        P("expert", SHARD),
        P("expert", SHARD),
    )
    return jax.shard_map(
        shards,
        mesh=torus,
        in_specs=placed,
        out_specs=(P("expert", None, None, SHARD), P("expert", None, None, None)),
        check_vma=False,
    )
```

```python
import jax
import jax.numpy as jnp
from jax import lax
from jax.experimental import pallas as pl
from jax.experimental.pallas import tpu as pltpu
from jax.sharding import Mesh
from jax.sharding import PartitionSpec as P

F32 = jnp.float32
BF16 = jnp.bfloat16

SHARD = ("x", "zh", "zl", "c")

outer_rate = 0.7

ROWS = 64
OWN = 224
LANES = 128
QUAD = 4
WIDE = QUAD * OWN
STEP = 32
TAIL = 16
REST = ROWS - TAIL

PIECE = ROWS + REST

NOTES = 16
FAR_NOTES = 8
TOP = 32767.0
DIGIT = 4096.0
MIDDLE = 32768.0
FINE = 8.0


def lane_group(shape):
    return lax.broadcasted_iota(jnp.int32, shape, 1) // STEP


def rolled(v, by):
    by %= LANES
    return jnp.concatenate([v[:, LANES - by :], v[:, : LANES - by]], axis=1) if by else v


def folded(res, k):
    free = QUAD - 1 - k
    tail = res[REST:]
    group = lane_group((TAIL, LANES))
    return jnp.concatenate(
        [jnp.where(group == free, rolled(tail, STEP * (m + 1)), res[m * TAIL : (m + 1) * TAIL]) for m in range(QUAD - 1)],
        axis=0,
    )


def unfolded(piece, k):
    free = QUAD - 1 - k
    group = lane_group((TAIL, LANES))
    tail = rolled(piece[:TAIL], -STEP)
    for m in range(1, QUAD - 1):
        moved = rolled(piece[m * TAIL : (m + 1) * TAIL], -STEP * (m + 1))
        tail = jnp.where(group == (free - m - 1) % QUAD, moved, tail)
    return jnp.concatenate([piece, tail], axis=0)


def own_parts(block, k):
    at = STEP * k
    res = [block[:, at + LANES :], jnp.zeros((ROWS, STEP), block.dtype), block[:, :at]]
    return block[:, at : at + LANES], folded(jnp.concatenate([r for r in res if r.shape[1]], axis=1), k)


def own_block(tile, piece, k):
    at = STEP * k
    res = unfolded(piece, k)
    parts = [res[:, LANES - at :] if k else res[:, :0], tile, res[:, : LANES - STEP - at]]
    return jnp.concatenate([p for p in parts if p.shape[1]], axis=1)


def as_bytes(count):
    high = count // 256
    return high.astype(F32), (count - 256 * high).astype(F32)


def in_rows(values, rows):
    row = lax.broadcasted_iota(jnp.int32, (rows, LANES), 0)
    out = jnp.zeros((rows, LANES), F32)
    for i, value in enumerate(values):
        out = jnp.where(row == i, value, out)
    return out


def digits(value):
    whole = jnp.floor(value)
    part = (value - whole) * DIGIT
    digit = jnp.floor(part)
    return whole, digit, jnp.floor((part - digit) * DIGIT)


def from_digits(whole, first, second):
    return whole + (first + second * (1 / DIGIT)) * (1 / DIGIT)


def coded(total):
    largest = jnp.maximum(jnp.max(jnp.abs(total), axis=0, keepdims=True), 1e-30)
    level = jnp.ceil(FINE * jnp.log2(largest))
    units = jnp.clip(jnp.round(total * (TOP * jnp.exp2(level * (-1 / FINE)))), -TOP, TOP)
    return short(units), level


def short(values):
    return values.astype(jnp.int32).astype(jnp.int16)


def wide(values):
    return values.astype(jnp.int32).astype(F32)


def decoded(units, level):
    return (jnp.exp2(level * (1 / FINE)) * (1 / TOP)) * wide(units)


def sort_kernel(core, tokens, steps, fast, keep, give):
    n_zl = keep.shape[1]
    group = lane_group((ROWS, LANES))

    def body(sides):
        for g in range(fast.shape[1] // WIDE):
            x, zh = divmod(g, keep.shape[2])
            lanes = [slice(g * WIDE + i * LANES, g * WIDE + (i + 1) * LANES) for i in range(2 * QUAD - 1)]
            odd = [fast[:, at].astype(F32) for at in lanes[1::2]]
            for k in range(QUAD):
                if k == 0:
                    res = odd[0]
                elif k == QUAD - 1:
                    res = odd[-1]
                else:
                    res = jnp.where(group >= QUAD - k, odd[k - 1], odd[k])
                zl, c = divmod(k, QUAD // n_zl)
                sides[c](x, zl, zh, fast[:, lanes[2 * k]], folded(res, k).astype(BF16))

    def kept(x, zl, zh, tile, rest):
        keep[x, zl, zh, :ROWS] = tile
        keep[x, zl, zh, ROWS:] = rest

    def given(x, zl, zh, tile, rest):
        at = ((x * n_zl + zl) * keep.shape[2] + zh) * PIECE
        give[at : at + ROWS] = tile
        give[at + ROWS : at + PIECE] = rest

    @pl.when(core[0, 0] == 0)
    def _():
        body((kept, given))

    @pl.when(core[0, 0] != 0)
    def _():
        body((given, kept))

    notes = in_rows((*as_bytes(tokens[0, 0]), *as_bytes(steps[0, 0])), NOTES)
    give[give.shape[0] - NOTES :] = notes.astype(BF16)


def pair_sum_kernel(tokens, steps, experts, keep, got, out):
    at = got.shape[0] - NOTES
    notes = got[at:].astype(F32)
    theirs = [256 * notes[2 * i : 2 * i + 1] + notes[2 * i + 1 : 2 * i + 2] for i in range(2)]
    mine = [jnp.full((1, LANES), count[0, 0].astype(F32)) for count in (tokens, steps)]
    share, other = mine[0] / mine[1], theirs[0] / theirs[1]
    everywhere = sum(experts[e, 0] for e in range(experts.shape[0])).astype(F32)
    counts = (mine[0] + theirs[0], mine[0] * mine[1] + theirs[0] * theirs[1], *digits(share + other), everywhere)
    n_zl, n_zh = keep.shape[1:3]
    for d in range(out.shape[0]):
        levels = []
        for zh in range(n_zh):
            at = (d * n_zh + zh) * PIECE
            mix = share * keep[d // n_zl, d % n_zl, zh].astype(F32) + other * got[at : at + PIECE].astype(F32)
            out[d, zh * PIECE : (zh + 1) * PIECE], level = coded(mix)
            levels.append(level)
        out[d, n_zh * PIECE :] = short(in_rows((*levels, *counts), NOTES))


def near_sum_kernel(got, out):
    n, n_zh = got.shape[0], out.shape[0]
    notes = [wide(got[s, n_zh * PIECE :]) for s in range(n)]
    tok, work, *qsum, everywhere = (sum(v[n_zh + i : n_zh + i + 1] for v in notes) for i in range(6))
    high = jnp.floor(work / DIGIT)
    far = (tok, high, work - DIGIT * high, everywhere - MIDDLE, *digits(from_digits(*qsum)))
    for zh in range(n_zh):
        piece = slice(zh * PIECE, (zh + 1) * PIECE)
        total = decoded(got[0, piece], notes[0][zh : zh + 1])
        for s in range(1, n):
            total = total + decoded(got[s, piece], notes[s][zh : zh + 1])
        out[zh, :PIECE], level = coded(total)
        out[zh, PIECE:] = short(in_rows((level, *far), FAR_NOTES))


def refresh_kernel(groups, place, got, slow, new_slow, copies):
    total = sums = None
    for s in range(got.shape[0]):
        notes = wide(got[s, PIECE:])
        part = decoded(got[s, :PIECE], notes[0:1])
        total, sums = (part, notes) if s == 0 else (total + part, sums + notes)
    tok = sums[1:2]
    work = DIGIT * sums[2:3] + sums[3:4]
    everywhere = sums[4:5] + MIDDLE * got.shape[0]
    qsum = from_digits(sums[5:6], sums[6:7], sums[7:8])
    rate = outer_rate * groups * work / (tok * everywhere)
    for k in range(QUAD):

        @pl.when(place[0, 0] == k)
        def _(k=k):
            mine = own_parts(slow[0, 0], k)
            tile = mine[0] + rate * (total[:ROWS] - qsum * mine[0])
            rest = mine[1] + rate * (total[ROWS:] - qsum * mine[1])
            new_slow[0, 0] = own_block(tile, rest, k)
            for i in range(copies.shape[0]):
                copies[i, :ROWS] = tile.astype(BF16)
                copies[i, ROWS:] = rest.astype(BF16)


def lay_out_kernel(core, own, other, out):
    def body(pieces):
        group = lane_group((ROWS, LANES))
        for zh in range(own.shape[2]):
            at = zh * WIDE
            for k in range(QUAD):
                out[:, at + 2 * k * LANES : at + (2 * k + 1) * LANES] = pieces[k % 2][0, k // 2, zh, :ROWS]
            res = [unfolded(pieces[k % 2][0, k // 2, zh, ROWS:].astype(F32), k) for k in range(QUAD)]
            for k in range(QUAD - 1):
                odd = jnp.where(group < QUAD - 1 - k, res[k], res[k + 1])
                out[:, at + (2 * k + 1) * LANES : at + (2 * k + 2) * LANES] = odd.astype(BF16)

    @pl.when(core[0, 0] == 0)
    def _():
        body((own, other))

    @pl.when(core[0, 0] != 0)
    def _():
        body((other, own))


def call(kernel, out_shape, **more):
    return pl.pallas_call(
        kernel,
        out_shape=out_shape,
        compiler_params=pltpu.CompilerParams(vmem_limit_bytes=48 * 2**20),
        **more,
    )


def struct(shape, dtype):
    return jax.ShapeDtypeStruct(shape, dtype)


def swap(pieces, axis):
    return lax.all_to_all(pieces, axis, split_axis=0, concat_axis=0, tiled=True)


SCALAR = pl.BlockSpec(memory_space=pltpu.SMEM)
WHOLE = pl.BlockSpec(memory_space=pltpu.VMEM)


def scalar(value):
    return value.astype(jnp.int32).reshape(1, 1)


def shards(fast_weights, slow_weights, step_counts, token_counts):
    size = {a: lax.axis_size(a) for a in SHARD}
    groups = lax.axis_size("expert")
    nx, nzh = size["x"], size["zh"]
    core = lax.axis_index("c")
    place = scalar(lax.axis_index("zl") * size["c"] + core)
    core = scalar(core)

    fast = fast_weights[0, 0, 0]
    half = fast.shape[1] // nx
    halves = pl.BlockSpec((ROWS, half), lambda x: (0, x))

    def by_x(*shape):
        return pl.BlockSpec((1, *shape[1:]), lambda x: (x, *(0 for _ in shape[1:])))

    plane = nx * size["zl"]
    spread = jnp.broadcast_to(token_counts, (groups * size["c"], 1))
    experts = swap(spread, ("expert", "c"))
    keep, give = call(
        sort_kernel,
        (
            struct((nx, size["zl"], nzh, PIECE, LANES), BF16),
            struct((plane * nzh * PIECE + NOTES, LANES), BF16),
        ),
        in_specs=[SCALAR, SCALAR, SCALAR, WHOLE],
    )(core, token_counts, step_counts, fast)
    got = lax.ppermute(give, "c", [(0, 1), (1, 0)])
    pairs = call(
        pair_sum_kernel,
        struct((plane, nzh * PIECE + NOTES, LANES), jnp.int16),
        in_specs=[SCALAR, SCALAR, SCALAR, WHOLE, WHOLE],
    )(token_counts, step_counts, experts, keep, got)
    got = swap(pairs, ("x", "zl"))
    sums = call(near_sum_kernel, struct((nzh, PIECE + FAR_NOTES, LANES), jnp.int16))(got)
    got = swap(sums, "zh")
    new_slow, copies = call(
        lambda *refs: refresh_kernel(groups, *refs),
        (struct(slow_weights.shape, F32), struct((nzh, PIECE, LANES), BF16)),
        in_specs=[SCALAR, WHOLE, WHOLE],
    )(place, got, slow_weights)

    column = swap(copies, "zh")
    own = swap(jnp.broadcast_to(column[None], (plane, *column.shape)), ("x", "zl"))
    other = lax.ppermute(own, "c", [(0, 1), (1, 0)])
    shape = (nx, size["zl"], *column.shape)
    reset = call(
        lay_out_kernel,
        struct(fast.shape, BF16),
        grid=(nx,),
        in_specs=[SCALAR, by_x(*shape), by_x(*shape)],
        out_specs=halves,
    )(core, own.reshape(shape), other.reshape(shape))
    return new_slow, reset[None, None]


def solution(mesh):
    torus = Mesh(
        mesh.devices.reshape(mesh.shape["expert"], 2, 8, 2, 2),
        ("expert", *SHARD),
    )
    placed = (
        P("expert", SHARD, None, None, None),
        P("expert", None, None, SHARD),
        P("expert", SHARD),
        P("expert", SHARD),
    )
    return jax.shard_map(
        shards,
        mesh=torus,
        in_specs=placed,
        out_specs=(P("expert", None, None, SHARD), P("expert", None, None, None)),
        check_vma=False,
    )
```

```python
import jax
import jax.numpy as jnp
from jax import lax
from jax.experimental import pallas as pl
from jax.experimental.pallas import tpu as pltpu
from jax.sharding import Mesh
from jax.sharding import PartitionSpec as P

F32 = jnp.float32
BF16 = jnp.bfloat16

SHARD = ("x", "zh", "zl", "c")

FAR = ("zh", "zl", "c")

outer_rate = 0.7

ROWS = 64
OWN = 224
LANES = 128
QUAD = 4
WIDE = QUAD * OWN
STEP = 32
TAIL = 16
REST = ROWS - TAIL

PIECE = ROWS + REST

NOTES = 16
FAR_NOTES = 8
TOP = 32767.0
DIGIT = 4096.0
MIDDLE = 32768.0
FINE = 8.0


SPREAD = (0, 4, 2, 6, 1, 5, 3, 7)


def member(at, k):
    return SPREAD[(at + 2 * k) % len(SPREAD)]


def position(zh, k):
    return (SPREAD[zh] - 2 * k) % len(SPREAD)


def swap_far(pieces):
    groups = [[member(at, k) * QUAD + k for at in range(len(SPREAD))] for k in range(QUAD)]
    return lax.all_to_all(pieces, FAR, split_axis=0, concat_axis=0, tiled=True, axis_index_groups=groups)


def lane_group(shape):
    return lax.broadcasted_iota(jnp.int32, shape, 1) // STEP


def rolled(v, by):
    by %= LANES
    return jnp.concatenate([v[:, LANES - by :], v[:, : LANES - by]], axis=1) if by else v


def folded(res, k):
    free = QUAD - 1 - k
    tail = res[REST:]
    group = lane_group((TAIL, LANES))
    return jnp.concatenate(
        [jnp.where(group == free, rolled(tail, STEP * (m + 1)), res[m * TAIL : (m + 1) * TAIL]) for m in range(QUAD - 1)],
        axis=0,
    )


def unfolded(piece, k):
    free = QUAD - 1 - k
    group = lane_group((TAIL, LANES))
    tail = rolled(piece[:TAIL], -STEP)
    for m in range(1, QUAD - 1):
        moved = rolled(piece[m * TAIL : (m + 1) * TAIL], -STEP * (m + 1))
        tail = jnp.where(group == (free - m - 1) % QUAD, moved, tail)
    return jnp.concatenate([piece, tail], axis=0)


def own_parts(block, k):
    at = STEP * k
    res = [block[:, at + LANES :], jnp.zeros((ROWS, STEP), block.dtype), block[:, :at]]
    return block[:, at : at + LANES], folded(jnp.concatenate([r for r in res if r.shape[1]], axis=1), k)


def own_block(tile, piece, k):
    at = STEP * k
    res = unfolded(piece, k)
    parts = [res[:, LANES - at :] if k else res[:, :0], tile, res[:, : LANES - STEP - at]]
    return jnp.concatenate([p for p in parts if p.shape[1]], axis=1)


def own_place():
    return lax.axis_index("zl") * 2 + lax.axis_index("c")


def in_rows(values, rows):
    row = lax.broadcasted_iota(jnp.int32, (rows, LANES), 0)
    out = jnp.zeros((rows, LANES), F32)
    for i, value in enumerate(values):
        out = jnp.where(row == i, value, out)
    return out


def digits(value):
    whole = jnp.floor(value)
    part = (value - whole) * DIGIT
    digit = jnp.floor(part)
    return whole, digit, jnp.floor((part - digit) * DIGIT)


def from_digits(whole, first, second):
    return whole + (first + second * (1 / DIGIT)) * (1 / DIGIT)


def coded(total):
    largest = jnp.maximum(jnp.max(jnp.abs(total), axis=0, keepdims=True), 1e-30)
    level = jnp.ceil(FINE * jnp.log2(largest))
    units = jnp.clip(jnp.round(total * (TOP * jnp.exp2(level * (-1 / FINE)))), -TOP, TOP)
    return short(units), level


def short(values):
    return values.astype(jnp.int32).astype(jnp.int16)


def wide(values):
    return values.astype(jnp.int32).astype(F32)


def decoded(units, level):
    return (jnp.exp2(level * (1 / FINE)) * (1 / TOP)) * wide(units)


def sort_kernel(fast, keep, give):
    n_zl = keep.shape[1]
    group = lane_group((ROWS, LANES))

    def body(sides):
        for g in range(fast.shape[1] // WIDE):
            x, zh = divmod(g, keep.shape[2])
            lanes = [slice(g * WIDE + i * LANES, g * WIDE + (i + 1) * LANES) for i in range(2 * QUAD - 1)]
            odd = [fast[:, at].astype(F32) for at in lanes[1::2]]
            for k in range(QUAD):
                if k == 0:
                    res = odd[0]
                elif k == QUAD - 1:
                    res = odd[-1]
                else:
                    res = jnp.where(group >= QUAD - k, odd[k - 1], odd[k])
                zl, c = divmod(k, QUAD // n_zl)
                sides[c][x, zl, zh, :ROWS] = fast[:, lanes[2 * k]]
                sides[c][x, zl, zh, ROWS:] = folded(res, k).astype(BF16)

    core = lax.axis_index("c")

    @pl.when(core == 0)
    def _():
        body((keep, give))

    @pl.when(core != 0)
    def _():
        body((give, keep))


def pair_sum_kernel(counts, keep, got, out):
    core = lax.axis_index("c")
    pair = lax.axis_index("expert") * 2
    of_core = [[counts[pair + c, i].astype(F32) for i in range(2)] for c in (core, 1 - core)]
    (tokens, steps), (tokens_2, steps_2) = ([jnp.full((1, LANES), v) for v in values] for values in of_core)
    share, other = tokens / steps, tokens_2 / steps_2
    everywhere = sum(counts[i, 0] for i in range(counts.shape[0])).astype(F32)
    sums = (tokens + tokens_2, tokens * steps + tokens_2 * steps_2, *digits(share + other), everywhere)
    n_zl, n_zh = keep.shape[1:3]
    for d in range(out.shape[0]):
        levels = []
        at = divmod(d, n_zl)
        for zh in range(n_zh):
            mix = share * keep[*at, zh].astype(F32) + other * got[*at, zh].astype(F32)
            out[d, zh * PIECE : (zh + 1) * PIECE], level = coded(mix)
            levels.append(level)
        out[d, n_zh * PIECE :] = short(in_rows((*levels, *sums), NOTES))


def near_sum_kernel(got, out):
    place = own_place()
    n, n_zh = got.shape[0], out.shape[0]
    notes = [wide(got[s, n_zh * PIECE :]) for s in range(n)]
    tok, work, *qsum, everywhere = (sum(v[n_zh + i : n_zh + i + 1] for v in notes) for i in range(6))
    high = jnp.floor(work / DIGIT)
    far = (tok, high, work - DIGIT * high, everywhere - MIDDLE, *digits(from_digits(*qsum)))
    for zh in range(n_zh):
        piece = slice(zh * PIECE, (zh + 1) * PIECE)
        total = decoded(got[0, piece], notes[0][zh : zh + 1])
        for s in range(1, n):
            total = total + decoded(got[s, piece], notes[s][zh : zh + 1])
        to = (SPREAD[zh] + (n_zh - 2) * place) % n_zh
        out[to, :PIECE], level = coded(total)
        out[to, PIECE:] = short(in_rows((level, *far), FAR_NOTES))


def refresh_kernel(groups, got, slow, new_slow, copies):
    total = sums = None
    for s in range(got.shape[0]):
        notes = wide(got[s, PIECE:])
        part = decoded(got[s, :PIECE], notes[0:1])
        total, sums = (part, notes) if s == 0 else (total + part, sums + notes)
    tok = sums[1:2]
    work = DIGIT * sums[2:3] + sums[3:4]
    everywhere = sums[4:5] + MIDDLE * got.shape[0]
    qsum = from_digits(sums[5:6], sums[6:7], sums[7:8])
    rate = outer_rate * groups * work / (tok * everywhere)
    place = own_place()
    for k in range(QUAD):

        @pl.when(place == k)
        def _(k=k):
            mine = own_parts(slow[0, 0], k)
            tile = mine[0] + rate * (total[:ROWS] - qsum * mine[0])
            rest = mine[1] + rate * (total[ROWS:] - qsum * mine[1])
            new_slow[0, 0] = own_block(tile, rest, k)
            for i in range(copies.shape[0]):
                copies[i, :ROWS] = tile.astype(BF16)
                copies[i, ROWS:] = rest.astype(BF16)


def lay_out_kernel(pieces, out):
    n_c, n_zl, n_zh = pieces.shape[0], pieces.shape[2], pieces.shape[3]
    group = lane_group((ROWS, LANES))
    for zh in range(n_zh):
        at = zh * WIDE
        res = []
        for k in range(QUAD):
            zl, c = divmod(k, n_c)
            piece = pieces.at[c, 0, zl, position(zh, k)]
            out[:, at + 2 * k * LANES : at + (2 * k + 1) * LANES] = piece[:ROWS]
            res.append(unfolded(piece[ROWS:].astype(F32), k))
        for k in range(QUAD - 1):
            odd = jnp.where(group < QUAD - 1 - k, res[k], res[k + 1])
            out[:, at + (2 * k + 1) * LANES : at + (2 * k + 2) * LANES] = odd.astype(BF16)


def call(kernel, out_shape, **more):
    return pl.pallas_call(
        kernel,
        out_shape=out_shape,
        compiler_params=pltpu.CompilerParams(vmem_limit_bytes=48 * 2**20),
        **more,
    )


def struct(shape, dtype):
    return jax.ShapeDtypeStruct(shape, dtype)


def swap(pieces, axis):
    return lax.all_to_all(pieces, axis, split_axis=0, concat_axis=0, tiled=True)


SCALAR = pl.BlockSpec(memory_space=pltpu.SMEM)
WHOLE = pl.BlockSpec(memory_space=pltpu.VMEM)


def shards(fast_weights, slow_weights, step_counts, token_counts):
    size = {a: lax.axis_size(a) for a in SHARD}
    groups = lax.axis_size("expert")
    nx, nzh = size["x"], size["zh"]
    fast = fast_weights[0, 0, 0]
    half = fast.shape[1] // nx
    halves = pl.BlockSpec((ROWS, half), lambda x: (0, x))

    plane = nx * size["zl"]
    pair = jnp.concatenate([token_counts, step_counts], axis=1)
    counts = swap(jnp.broadcast_to(pair, (groups * size["c"], 2)), ("expert", "c"))
    shape = (nx, size["zl"], nzh, PIECE, LANES)
    keep, give = call(sort_kernel, (struct(shape, BF16), struct(shape, BF16)))(fast)
    got = lax.ppermute(give, "c", [(0, 1), (1, 0)])
    pairs = call(
        pair_sum_kernel,
        struct((plane, nzh * PIECE + NOTES, LANES), jnp.int16),
        in_specs=[SCALAR, WHOLE, WHOLE],
    )(counts, keep, got)
    got = swap(pairs, ("x", "zl"))
    sums = call(near_sum_kernel, struct((nzh, PIECE + FAR_NOTES, LANES), jnp.int16))(got)
    got = swap_far(sums)
    new_slow, copies = call(
        lambda *refs: refresh_kernel(groups, *refs),
        (struct(slow_weights.shape, F32), struct((nzh, PIECE, LANES), BF16)),
    )(got, slow_weights)

    column = swap_far(copies)
    own = swap(jnp.broadcast_to(column[None], (plane, *column.shape)), ("x", "zl"))
    both = swap(jnp.broadcast_to(own[None], (size["c"], *own.shape)), "c").reshape(size["c"], *shape)
    reset = call(
        lay_out_kernel,
        struct(fast.shape, BF16),
        grid=(nx,),
        in_specs=[pl.BlockSpec((size["c"], 1, *shape[1:]), lambda x: (0, x, 0, 0, 0, 0))],
        out_specs=halves,
    )(both)
    return new_slow, reset[None, None]


def solution(mesh):
    torus = Mesh(
        mesh.devices.reshape(mesh.shape["expert"], 2, 8, 2, 2),
        ("expert", *SHARD),
    )
    placed = (
        P("expert", SHARD, None, None, None),
        P("expert", None, None, SHARD),
        P("expert", SHARD),
        P("expert", SHARD),
    )
    return jax.shard_map(
        shards,
        mesh=torus,
        in_specs=placed,
        out_specs=(P("expert", None, None, SHARD), P("expert", None, None, None)),
        check_vma=False,
    )
```

```python
import jax
import jax.numpy as jnp
from jax import lax
from jax.experimental import pallas as pl
from jax.experimental.pallas import tpu as pltpu
from jax.sharding import Mesh
from jax.sharding import PartitionSpec as P

F32 = jnp.float32
BF16 = jnp.bfloat16

SHARD = ("x", "zh", "zl", "c")

FAR = ("zh", "zl", "c")

outer_rate = 0.7

ROWS = 64
OWN = 224
LANES = 128
QUAD = 4
WIDE = QUAD * OWN
STEP = 32
TAIL = 16
REST = ROWS - TAIL

PIECE = ROWS + REST

NOTES = 16
FAR_NOTES = 8
TOP = 32767.0
DIGIT = 4096.0
FINE = 8.0


SPREAD = (0, 4, 2, 6, 1, 5, 3, 7)


def member(at, k):
    return SPREAD[(at + 2 * k) % len(SPREAD)]


def position(zh, k):
    return (SPREAD[zh] - 2 * k) % len(SPREAD)


def swap_far(pieces):
    groups = [[member(at, k) * QUAD + k for at in range(len(SPREAD))] for k in range(QUAD)]
    return lax.all_to_all(pieces, FAR, split_axis=0, concat_axis=0, tiled=True, axis_index_groups=groups)


def lane_group(shape):
    return lax.broadcasted_iota(jnp.int32, shape, 1) // STEP


def rolled(v, by):
    by %= LANES
    return jnp.concatenate([v[:, LANES - by :], v[:, : LANES - by]], axis=1) if by else v


def folded(res, k):
    free = QUAD - 1 - k
    tail = res[REST:]
    group = lane_group((TAIL, LANES))
    return jnp.concatenate(
        [jnp.where(group == free, rolled(tail, STEP * (m + 1)), res[m * TAIL : (m + 1) * TAIL]) for m in range(QUAD - 1)],
        axis=0,
    )


def unfolded(piece, k):
    free = QUAD - 1 - k
    group = lane_group((TAIL, LANES))
    tail = rolled(piece[:TAIL], -STEP)
    for m in range(1, QUAD - 1):
        moved = rolled(piece[m * TAIL : (m + 1) * TAIL], -STEP * (m + 1))
        tail = jnp.where(group == (free - m - 1) % QUAD, moved, tail)
    return jnp.concatenate([piece, tail], axis=0)


def own_parts(block, k):
    at = STEP * k
    res = [block[:, at + LANES :], jnp.zeros((ROWS, STEP), block.dtype), block[:, :at]]
    return block[:, at : at + LANES], folded(jnp.concatenate([r for r in res if r.shape[1]], axis=1), k)


def own_block(tile, piece, k):
    at = STEP * k
    res = unfolded(piece, k)
    parts = [res[:, LANES - at :] if k else res[:, :0], tile, res[:, : LANES - STEP - at]]
    return jnp.concatenate([p for p in parts if p.shape[1]], axis=1)


def as_bytes(count):
    high = jnp.floor(count * (1 / 256))
    return high, count - 256 * high


def own_place():
    return lax.axis_index("zl") * 2 + lax.axis_index("c")


def in_rows(values, rows):
    row = lax.broadcasted_iota(jnp.int32, (rows, LANES), 0)
    out = jnp.zeros((rows, LANES), F32)
    for i, value in enumerate(values):
        out = jnp.where(row == i, value, out)
    return out


def digits(value):
    whole = jnp.floor(value)
    part = (value - whole) * DIGIT
    digit = jnp.floor(part)
    return whole, digit, jnp.floor((part - digit) * DIGIT)


def from_digits(whole, first, second):
    return whole + (first + second * (1 / DIGIT)) * (1 / DIGIT)


def coded(total):
    largest = jnp.maximum(jnp.max(jnp.abs(total), axis=0, keepdims=True), 1e-30)
    level = jnp.ceil(FINE * jnp.log2(largest))
    units = jnp.clip(jnp.round(total * (TOP * jnp.exp2(level * (-1 / FINE)))), -TOP, TOP)
    return short(units), level


def short(values):
    return values.astype(jnp.int32).astype(jnp.int16)


def wide(values):
    return values.astype(jnp.int32).astype(F32)


def decoded(units, level):
    return (jnp.exp2(level * (1 / FINE)) * (1 / TOP)) * wide(units)


def sort_kernel(tokens, steps, fast, out):
    n_c = out.shape[0]
    n_zl = QUAD // n_c
    n_zh = len(SPREAD)
    group = lane_group((ROWS, LANES))
    for g in range(fast.shape[1] // WIDE):
        x, zh = divmod(g, n_zh)
        lanes = [slice(g * WIDE + i * LANES, g * WIDE + (i + 1) * LANES) for i in range(2 * QUAD - 1)]
        odd = [fast[:, at].astype(F32) for at in lanes[1::2]]
        for k in range(QUAD):
            if k == 0:
                res = odd[0]
            elif k == QUAD - 1:
                res = odd[-1]
            else:
                res = jnp.where(group >= QUAD - k, odd[k - 1], odd[k])
            zl, c = divmod(k, n_c)
            at = ((x * n_zl + zl) * n_zh + zh) * PIECE
            out[c, at : at + ROWS] = fast[:, lanes[2 * k]]
            out[c, at + ROWS : at + PIECE] = folded(res, k).astype(BF16)
    counts = [jnp.broadcast_to(v[...].astype(F32), (1, LANES)) for v in (tokens, steps)]
    notes = in_rows([v for count in counts for v in as_bytes(count)], NOTES).astype(BF16)
    for c in range(n_c):
        out[c, out.shape[1] - NOTES :] = notes


def pair_sum_kernel(got, out):
    rows = got.shape[1] - NOTES
    notes = [got[c, rows:].astype(F32) for c in range(got.shape[0])]
    counts = [[256 * v[2 * i : 2 * i + 1] + v[2 * i + 1 : 2 * i + 2] for i in range(2)] for v in notes]
    shares = [tokens / steps for tokens, steps in counts]
    tok = sum(tokens for tokens, _ in counts)
    sums = (tok, sum(tokens * steps for tokens, steps in counts), *digits(sum(shares)))
    n_zh = len(SPREAD)
    for d in range(out.shape[0]):
        levels = []
        for zh in range(n_zh):
            at = (d * n_zh + zh) * PIECE
            mix = sum(share * got[c, at : at + PIECE].astype(F32) for c, share in enumerate(shares))
            out[d, zh * PIECE : (zh + 1) * PIECE], level = coded(mix)
            levels.append(level)
        out[d, n_zh * PIECE :] = short(in_rows((*levels, *sums), NOTES))


def near_sum_kernel(got, out):
    place = own_place()
    n, n_zh = got.shape[0], out.shape[0]
    notes = [wide(got[s, n_zh * PIECE :]) for s in range(n)]
    tok, work, *qsum = (sum(v[n_zh + i : n_zh + i + 1] for v in notes) for i in range(5))
    high = jnp.floor(work / DIGIT)
    far = (tok, high, work - DIGIT * high, *digits(from_digits(*qsum)))
    for zh in range(n_zh):
        piece = slice(zh * PIECE, (zh + 1) * PIECE)
        total = decoded(got[0, piece], notes[0][zh : zh + 1])
        for s in range(1, n):
            total = total + decoded(got[s, piece], notes[s][zh : zh + 1])
        to = (SPREAD[zh] + (n_zh - 2) * place) % n_zh
        out[to, :PIECE], level = coded(total)
        out[to, PIECE:] = short(in_rows((level, *far), FAR_NOTES))


def tokens_kernel(got, out):
    tok = sum(wide(got[s, PIECE:])[1:2] for s in range(got.shape[0]))
    for e in range(out.shape[0]):
        out[e] = tok


def for_own_place(body):
    place = own_place()
    for k in range(QUAD):

        @pl.when(place == k)
        def _(k=k):
            body(k)


def far_sum_kernel(got, slow, mine, step, pace):
    total = sums = None
    for s in range(got.shape[0]):
        notes = wide(got[s, PIECE:])
        part = decoded(got[s, :PIECE], notes[0:1])
        total, sums = (part, notes) if s == 0 else (total + part, sums + notes)
    work = DIGIT * sums[2:3] + sums[3:4]
    qsum = from_digits(sums[4:5], sums[5:6], sums[6:7])
    pace[0:1] = work
    pace[1:2] = sums[1:2]

    def body(k):
        for rows, part in zip((slice(0, ROWS), slice(ROWS, PIECE)), own_parts(slow[0, 0], k)):
            mine[rows] = part
            step[rows] = total[rows] - qsum * part

    for_own_place(body)


def refresh_kernel(experts, mine, step, pace, new_slow, copies):
    groups = experts.shape[0]
    everywhere = sum(experts[e] for e in range(groups))
    rate = outer_rate * groups * pace[0:1] / (pace[1:2] * everywhere)
    new = mine[...] + rate * step[...]
    for i in range(copies.shape[0]):
        copies[i] = new.astype(BF16)

    def body(k):
        new_slow[0, 0] = own_block(new[:ROWS], new[ROWS:], k)

    for_own_place(body)


def lay_out_kernel(pieces, out):
    n_c, n_zl, n_zh = pieces.shape[0], pieces.shape[2], pieces.shape[3]
    group = lane_group((ROWS, LANES))
    for zh in range(n_zh):
        at = zh * WIDE
        res = []
        for k in range(QUAD):
            zl, c = divmod(k, n_c)
            piece = pieces.at[c, 0, zl, position(zh, k)]
            out[:, at + 2 * k * LANES : at + (2 * k + 1) * LANES] = piece[:ROWS]
            res.append(unfolded(piece[ROWS:].astype(F32), k))
        for k in range(QUAD - 1):
            odd = jnp.where(group < QUAD - 1 - k, res[k], res[k + 1])
            out[:, at + (2 * k + 1) * LANES : at + (2 * k + 2) * LANES] = odd.astype(BF16)


def call(kernel, out_shape, **more):
    return pl.pallas_call(
        kernel,
        out_shape=out_shape,
        compiler_params=pltpu.CompilerParams(vmem_limit_bytes=48 * 2**20),
        **more,
    )


def struct(shape, dtype):
    return jax.ShapeDtypeStruct(shape, dtype)


def swap(pieces, axis):
    return lax.all_to_all(pieces, axis, split_axis=0, concat_axis=0, tiled=True)


def shards(fast_weights, slow_weights, step_counts, token_counts):
    size = {a: lax.axis_size(a) for a in SHARD}
    groups = lax.axis_size("expert")
    nx, nzh = size["x"], size["zh"]
    fast = fast_weights[0, 0, 0]
    half = fast.shape[1] // nx
    halves = pl.BlockSpec((ROWS, half), lambda x: (0, x))

    plane = nx * size["zl"]
    shape = (nx, size["zl"], nzh, PIECE, LANES)
    raw = call(sort_kernel, struct((size["c"], plane * nzh * PIECE + NOTES, LANES), BF16))(
        token_counts, step_counts, fast
    )
    got = swap(raw, "c")
    got = swap(call(pair_sum_kernel, struct((plane, nzh * PIECE + NOTES, LANES), jnp.int16))(got), ("x", "zl"))
    got = swap_far(call(near_sum_kernel, struct((nzh, PIECE + FAR_NOTES, LANES), jnp.int16))(got))
    experts = swap(call(tokens_kernel, struct((groups, 1, LANES), F32))(got), "expert")
    block = struct((PIECE, LANES), F32)
    terms = call(far_sum_kernel, (block, block, struct((FAR_NOTES, LANES), F32)))(got, slow_weights)
    new_slow, copies = call(
        refresh_kernel, (struct(slow_weights.shape, F32), struct((nzh, PIECE, LANES), BF16))
    )(experts, *terms)

    column = swap_far(copies)
    own = swap(jnp.broadcast_to(column[None], (plane, *column.shape)), ("x", "zl"))
    both = swap(jnp.broadcast_to(own[None], (size["c"], *own.shape)), "c").reshape(size["c"], *shape)
    reset = call(
        lay_out_kernel,
        struct(fast.shape, BF16),
        grid=(nx,),
        in_specs=[pl.BlockSpec((size["c"], 1, *shape[1:]), lambda x: (0, x, 0, 0, 0, 0))],
        out_specs=halves,
    )(both)
    return new_slow, reset[None, None]


def solution(mesh):
    torus = Mesh(
        mesh.devices.reshape(mesh.shape["expert"], 2, 8, 2, 2),
        ("expert", *SHARD),
    )
    placed = (
        P("expert", SHARD, None, None, None),
        P("expert", None, None, SHARD),
        P("expert", SHARD),
        P("expert", SHARD),
    )
    return jax.shard_map(
        shards,
        mesh=torus,
        in_specs=placed,
        out_specs=(P("expert", None, None, SHARD), P("expert", None, None, None)),
        check_vma=False,
    )
```

```python
import jax
import jax.numpy as jnp
from jax import lax
from jax.experimental import pallas as pl
from jax.experimental.pallas import tpu as pltpu
from jax.sharding import Mesh
from jax.sharding import PartitionSpec as P

F32 = jnp.float32
BF16 = jnp.bfloat16

SHARD = ("x", "zh", "zl", "c")

outer_rate = 0.7

ROWS = 64
OWN = 224
LANES = 128
QUAD = 4
WIDE = QUAD * OWN
STEP = 32
TAIL = 16
REST = ROWS - TAIL

PIECE = ROWS + REST

NOTES = 16
FAR_NOTES = 8
TOP = 32767.0
DIGIT = 4096.0
MIDDLE = 32768.0
FINE = 8.0


def lane_group(shape):
    return lax.broadcasted_iota(jnp.int32, shape, 1) // STEP


def rolled(v, by):
    by %= LANES
    return jnp.concatenate([v[:, LANES - by :], v[:, : LANES - by]], axis=1) if by else v


def folded(res, k):
    free = QUAD - 1 - k
    tail = res[REST:]
    group = lane_group((TAIL, LANES))
    return jnp.concatenate(
        [jnp.where(group == free, rolled(tail, STEP * (m + 1)), res[m * TAIL : (m + 1) * TAIL]) for m in range(QUAD - 1)],
        axis=0,
    )


def unfolded(piece, k):
    free = QUAD - 1 - k
    group = lane_group((TAIL, LANES))
    tail = rolled(piece[:TAIL], -STEP)
    for m in range(1, QUAD - 1):
        moved = rolled(piece[m * TAIL : (m + 1) * TAIL], -STEP * (m + 1))
        tail = jnp.where(group == (free - m - 1) % QUAD, moved, tail)
    return jnp.concatenate([piece, tail], axis=0)


def own_parts(block, k):
    at = STEP * k
    res = [block[:, at + LANES :], jnp.zeros((ROWS, STEP), block.dtype), block[:, :at]]
    return block[:, at : at + LANES], folded(jnp.concatenate([r for r in res if r.shape[1]], axis=1), k)


def own_block(tile, piece, k):
    at = STEP * k
    res = unfolded(piece, k)
    parts = [res[:, LANES - at :] if k else res[:, :0], tile, res[:, : LANES - STEP - at]]
    return jnp.concatenate([p for p in parts if p.shape[1]], axis=1)


def own_place():
    return lax.axis_index("zl") * 2 + lax.axis_index("c")


def for_core(first, second):
    core = lax.axis_index("c")
    pl.when(core == 0)(first)
    pl.when(core != 0)(second)


def in_rows(values, rows):
    row = lax.broadcasted_iota(jnp.int32, (rows, LANES), 0)
    out = jnp.zeros((rows, LANES), F32)
    for i, value in enumerate(values):
        out = jnp.where(row == i, value, out)
    return out


def digits(value):
    whole = jnp.floor(value)
    part = (value - whole) * DIGIT
    digit = jnp.floor(part)
    return whole, digit, jnp.floor((part - digit) * DIGIT)


def from_digits(whole, first, second):
    return whole + (first + second * (1 / DIGIT)) * (1 / DIGIT)


def coded(total):
    largest = jnp.maximum(jnp.max(jnp.abs(total), axis=0, keepdims=True), 1e-30)
    level = jnp.ceil(FINE * jnp.log2(largest))
    units = jnp.clip(jnp.round(total * (TOP * jnp.exp2(level * (-1 / FINE)))), -TOP, TOP)
    return short(units), level


def short(values):
    return values.astype(jnp.int32).astype(jnp.int16)


def wide(values):
    return values.astype(jnp.int32).astype(F32)


def decoded(units, level):
    return (jnp.exp2(level * (1 / FINE)) * (1 / TOP)) * wide(units)


def own_pieces(fast, g, core):
    group = lane_group((ROWS, LANES))
    lanes = [slice(g * WIDE + i * LANES, g * WIDE + (i + 1) * LANES) for i in range(2 * QUAD - 1)]
    odd = [fast[:, at].astype(F32) for at in lanes[1::2]]
    pieces = []
    for k in range(core, QUAD, 2):
        if k == 0:
            res = odd[0]
        elif k == QUAD - 1:
            res = odd[-1]
        else:
            res = jnp.where(group >= QUAD - k, odd[k - 1], odd[k])
        pieces.append((fast[:, lanes[2 * k]].astype(F32), folded(res, k)))
    return pieces


def sort_kernel(fast, keep):
    nx, n_zl, n_zh = keep.shape[:3]

    def body(core):
        for g in range(nx * n_zh):
            x, zh = divmod(g, n_zh)
            for zl, (tile, rest) in enumerate(own_pieces(fast, g, core)):
                keep[x, zl, zh, :ROWS] = tile.astype(BF16)
                keep[x, zl, zh, ROWS:] = rest.astype(BF16)

    for_core(lambda: body(0), lambda: body(1))


def pair_sum_kernel(counts, keep, other, out):
    nx, n_zl, n_zh = keep.shape[:3]

    def body(core):
        pair = lax.axis_index("expert") * 2
        tokens, steps = ([jnp.full((1, LANES), counts[pair + c, i].astype(F32)) for c in (core, 1 - core)] for i in range(2))
        shares = [t / n for t, n in zip(tokens, steps)]
        everywhere = sum(counts[i, 0] for i in range(counts.shape[0])).astype(F32)
        work = sum(t * n for t, n in zip(tokens, steps))
        sums = (sum(tokens), work, *digits(sum(shares)), everywhere)
        levels = [[] for _ in range(out.shape[0])]
        for g in range(nx * n_zh):
            x, zh = divmod(g, n_zh)
            for zl, parts in enumerate(own_pieces(other, g, core)):
                d = x * n_zl + zl
                mix = shares[0] * keep[x, zl, zh].astype(F32) + shares[1] * jnp.concatenate(parts, axis=0)
                out[d, zh * PIECE : (zh + 1) * PIECE], level = coded(mix)
                levels[d].append(level)
        for d in range(out.shape[0]):
            out[d, n_zh * PIECE :] = short(in_rows((*levels[d], *sums), NOTES))

    for_core(lambda: body(0), lambda: body(1))


def near_sum_kernel(got, out):
    n, n_zh = got.shape[0], out.shape[0]
    notes = [wide(got[s, n_zh * PIECE :]) for s in range(n)]
    tok, work, *qsum, everywhere = (sum(v[n_zh + i : n_zh + i + 1] for v in notes) for i in range(6))
    high = jnp.floor(work / DIGIT)
    far = (tok, high, work - DIGIT * high, everywhere - MIDDLE, *digits(from_digits(*qsum)))
    for zh in range(n_zh):
        piece = slice(zh * PIECE, (zh + 1) * PIECE)
        total = decoded(got[0, piece], notes[0][zh : zh + 1])
        for s in range(1, n):
            total = total + decoded(got[s, piece], notes[s][zh : zh + 1])
        out[zh, :PIECE], level = coded(total)
        out[zh, PIECE:] = short(in_rows((level, *far), FAR_NOTES))


def refresh_kernel(groups, got, slow, new_slow, copies):
    total = sums = None
    for s in range(got.shape[0]):
        notes = wide(got[s, PIECE:])
        part = decoded(got[s, :PIECE], notes[0:1])
        total, sums = (part, notes) if s == 0 else (total + part, sums + notes)
    tok = sums[1:2]
    work = DIGIT * sums[2:3] + sums[3:4]
    everywhere = sums[4:5] + MIDDLE * got.shape[0]
    qsum = from_digits(sums[5:6], sums[6:7], sums[7:8])
    rate = outer_rate * groups * work / (tok * everywhere)
    place = own_place()
    for k in range(QUAD):

        @pl.when(place == k)
        def _(k=k):
            mine = own_parts(slow[0, 0], k)
            tile = mine[0] + rate * (total[:ROWS] - qsum * mine[0])
            rest = mine[1] + rate * (total[ROWS:] - qsum * mine[1])
            new_slow[0, 0] = own_block(tile, rest, k)
            for i in range(copies.shape[0]):
                copies[i, :ROWS] = tile.astype(BF16)
                copies[i, ROWS:] = rest.astype(BF16)


def lay_out_kernel(own, other, out):
    def body(pieces):
        group = lane_group((ROWS, LANES))
        for zh in range(own.shape[2]):
            at = zh * WIDE
            for k in range(QUAD):
                out[:, at + 2 * k * LANES : at + (2 * k + 1) * LANES] = pieces[k % 2][0, k // 2, zh, :ROWS]
            res = [unfolded(pieces[k % 2][0, k // 2, zh, ROWS:].astype(F32), k) for k in range(QUAD)]
            for k in range(QUAD - 1):
                odd = jnp.where(group < QUAD - 1 - k, res[k], res[k + 1])
                out[:, at + (2 * k + 1) * LANES : at + (2 * k + 2) * LANES] = odd.astype(BF16)

    for_core(lambda: body((own, other)), lambda: body((other, own)))


def call(kernel, out_shape, **more):
    return pl.pallas_call(
        kernel,
        out_shape=out_shape,
        compiler_params=pltpu.CompilerParams(vmem_limit_bytes=48 * 2**20),
        **more,
    )


def struct(shape, dtype):
    return jax.ShapeDtypeStruct(shape, dtype)


def swap(pieces, axis):
    return lax.all_to_all(pieces, axis, split_axis=0, concat_axis=0, tiled=True)


SCALAR = pl.BlockSpec(memory_space=pltpu.SMEM)
WHOLE = pl.BlockSpec(memory_space=pltpu.VMEM)


def shards(fast_weights, slow_weights, step_counts, token_counts):
    size = {a: lax.axis_size(a) for a in SHARD}
    groups = lax.axis_size("expert")
    nx, nzh = size["x"], size["zh"]
    fast = fast_weights[0, 0, 0]
    half = fast.shape[1] // nx
    halves = pl.BlockSpec((ROWS, half), lambda x: (0, x))

    plane = nx * size["zl"]
    pair = jnp.concatenate([token_counts, step_counts], axis=1)
    counts = swap(jnp.broadcast_to(pair, (groups * size["c"], 2)), ("expert", "c"))
    other = lax.ppermute(fast, "c", [(0, 1), (1, 0)])
    shape = (nx, size["zl"], nzh, PIECE, LANES)
    keep = call(sort_kernel, struct(shape, BF16))(fast)
    pairs = call(
        pair_sum_kernel,
        struct((plane, nzh * PIECE + NOTES, LANES), jnp.int16),
        in_specs=[SCALAR, WHOLE, WHOLE],
    )(counts, keep, other)
    got = swap(pairs, ("x", "zl"))
    sums = call(near_sum_kernel, struct((nzh, PIECE + FAR_NOTES, LANES), jnp.int16))(got)
    got = swap(sums, "zh")
    new_slow, copies = call(
        lambda *refs: refresh_kernel(groups, *refs),
        (struct(slow_weights.shape, F32), struct((nzh, PIECE, LANES), BF16)),
    )(got, slow_weights)

    column = swap(copies, "zh")
    own = swap(jnp.broadcast_to(column[None], (plane, *column.shape)), ("x", "zl"))
    other = lax.ppermute(own, "c", [(0, 1), (1, 0)])
    planes = pl.BlockSpec((1, *shape[1:]), lambda x: (x, 0, 0, 0, 0))
    reset = call(
        lay_out_kernel,
        struct(fast.shape, BF16),
        grid=(nx,),
        in_specs=[planes, planes],
        out_specs=halves,
    )(own.reshape(shape), other.reshape(shape))
    return new_slow, reset[None, None]


def solution(mesh):
    torus = Mesh(
        mesh.devices.reshape(mesh.shape["expert"], 2, 8, 2, 2),
        ("expert", *SHARD),
    )
    placed = (
        P("expert", SHARD, None, None, None),
        P("expert", None, None, SHARD),
        P("expert", SHARD),
        P("expert", SHARD),
    )
    return jax.shard_map(
        shards,
        mesh=torus,
        in_specs=placed,
        out_specs=(P("expert", None, None, SHARD), P("expert", None, None, None)),
        check_vma=False,
    )
```

```python
import jax
import jax.numpy as jnp
from jax import lax
from jax.experimental import pallas as pl
from jax.experimental.pallas import tpu as pltpu
from jax.sharding import Mesh
from jax.sharding import PartitionSpec as P

F32 = jnp.float32
BF16 = jnp.bfloat16

SHARD = ("x", "zh", "zl", "c")

outer_rate = 0.7

ROWS = 64
OWN = 224
LANES = 128
QUAD = 4
WIDE = QUAD * OWN
STEP = 32
TAIL = 16
REST = ROWS - TAIL

PIECE = ROWS + REST

NOTES = 16
FAR_NOTES = 8
FIELD = 2**16
TOP = 32767.0
DIGIT = 4096.0
MIDDLE = 32768.0
FINE = 8.0


def lane_group(shape):
    return lax.broadcasted_iota(jnp.int32, shape, 1) // STEP


def rolled(v, by):
    by %= LANES
    return jnp.concatenate([v[:, LANES - by :], v[:, : LANES - by]], axis=1) if by else v


def folded(res, k):
    free = QUAD - 1 - k
    tail = res[REST:]
    group = lane_group((TAIL, LANES))
    return jnp.concatenate(
        [jnp.where(group == free, rolled(tail, STEP * (m + 1)), res[m * TAIL : (m + 1) * TAIL]) for m in range(QUAD - 1)],
        axis=0,
    )


def unfolded(piece, k):
    free = QUAD - 1 - k
    group = lane_group((TAIL, LANES))
    tail = rolled(piece[:TAIL], -STEP)
    for m in range(1, QUAD - 1):
        moved = rolled(piece[m * TAIL : (m + 1) * TAIL], -STEP * (m + 1))
        tail = jnp.where(group == (free - m - 1) % QUAD, moved, tail)
    return jnp.concatenate([piece, tail], axis=0)


def own_parts(block, k):
    at = STEP * k
    res = [block[:, at + LANES :], jnp.zeros((ROWS, STEP), block.dtype), block[:, :at]]
    return block[:, at : at + LANES], folded(jnp.concatenate([r for r in res if r.shape[1]], axis=1), k)


def own_block(tile, piece, k):
    at = STEP * k
    res = unfolded(piece, k)
    parts = [res[:, LANES - at :] if k else res[:, :0], tile, res[:, : LANES - STEP - at]]
    return jnp.concatenate([p for p in parts if p.shape[1]], axis=1)


def own_place():
    return lax.axis_index("zl") * 2 + lax.axis_index("c")


def for_core(first, second):
    core = lax.axis_index("c")
    pl.when(core == 0)(first)
    pl.when(core != 0)(second)


def in_rows(values, rows):
    row = lax.broadcasted_iota(jnp.int32, (rows, LANES), 0)
    out = jnp.zeros((rows, LANES), F32)
    for i, value in enumerate(values):
        out = jnp.where(row == i, value, out)
    return out


def digits(value):
    whole = jnp.floor(value)
    part = (value - whole) * DIGIT
    digit = jnp.floor(part)
    return whole, digit, jnp.floor((part - digit) * DIGIT)


def from_digits(whole, first, second):
    return whole + (first + second * (1 / DIGIT)) * (1 / DIGIT)


def coded(total):
    largest = jnp.maximum(jnp.max(jnp.abs(total), axis=0, keepdims=True), 1e-30)
    level = jnp.ceil(FINE * jnp.log2(largest))
    units = jnp.clip(jnp.round(total * (TOP * jnp.exp2(level * (-1 / FINE)))), -TOP, TOP)
    return short(units), level


def short(values):
    return values.astype(jnp.int32).astype(jnp.int16)


def wide(values):
    return values.astype(jnp.int32).astype(F32)


def decoded(units, level):
    return (jnp.exp2(level * (1 / FINE)) * (1 / TOP)) * wide(units)


def fields(both):
    return both // FIELD, both % FIELD


def own_pieces(fast, g, core):
    group = lane_group((ROWS, LANES))
    lanes = [slice(g * WIDE + i * LANES, g * WIDE + (i + 1) * LANES) for i in range(2 * QUAD - 1)]
    odd = [fast[:, at].astype(F32) for at in lanes[1::2]]
    pieces = []
    for k in range(core, QUAD, 2):
        if k == 0:
            res = odd[0]
        elif k == QUAD - 1:
            res = odd[-1]
        else:
            res = jnp.where(group >= QUAD - k, odd[k - 1], odd[k])
        pieces.append((fast[:, lanes[2 * k]].astype(F32), folded(res, k)))
    return pieces


def sort_kernel(fast, keep):
    nx, n_zl, n_zh = keep.shape[:3]

    def body(core):
        for g in range(nx * n_zh):
            x, zh = divmod(g, n_zh)
            for zl, (tile, rest) in enumerate(own_pieces(fast, g, core)):
                keep[x, zl, zh, :ROWS] = tile.astype(BF16)
                keep[x, zl, zh, ROWS:] = rest.astype(BF16)

    for_core(lambda: body(0), lambda: body(1))


def pair_sum_kernel(counts, keep, other, out):
    nx, n_zl, n_zh = keep.shape[:3]

    def body(core):
        pair = lax.axis_index("expert") * 2
        both = [counts[pair + c, 0] for c in (core, 1 - core)]
        tokens, steps = ([jnp.full((1, LANES), v.astype(F32)) for v in f] for f in zip(*map(fields, both)))
        shares = [t / n for t, n in zip(tokens, steps)]
        everywhere = sum(fields(counts[i, 0])[0] for i in range(counts.shape[0])).astype(F32)
        work = sum(t * n for t, n in zip(tokens, steps))
        sums = (sum(tokens), work, *digits(sum(shares)), everywhere)
        levels = [[] for _ in range(out.shape[0])]
        for g in range(nx * n_zh):
            x, zh = divmod(g, n_zh)
            for zl, parts in enumerate(own_pieces(other, g, core)):
                d = x * n_zl + zl
                mix = shares[0] * keep[x, zl, zh].astype(F32) + shares[1] * jnp.concatenate(parts, axis=0)
                out[d, zh * PIECE : (zh + 1) * PIECE], level = coded(mix)
                levels[d].append(level)
        for d in range(out.shape[0]):
            out[d, n_zh * PIECE :] = short(in_rows((*levels[d], *sums), NOTES))

    for_core(lambda: body(0), lambda: body(1))


def near_sum_kernel(got, out):
    n, n_zh = got.shape[0], out.shape[0]
    notes = [wide(got[s, n_zh * PIECE :]) for s in range(n)]
    tok, work, *qsum, everywhere = (sum(v[n_zh + i : n_zh + i + 1] for v in notes) for i in range(6))
    high = jnp.floor(work / DIGIT)
    far = (tok, high, work - DIGIT * high, everywhere - MIDDLE, *digits(from_digits(*qsum)))
    for zh in range(n_zh):
        piece = slice(zh * PIECE, (zh + 1) * PIECE)
        total = decoded(got[0, piece], notes[0][zh : zh + 1])
        for s in range(1, n):
            total = total + decoded(got[s, piece], notes[s][zh : zh + 1])
        out[zh, :PIECE], level = coded(total)
        out[zh, PIECE:] = short(in_rows((level, *far), FAR_NOTES))


def refresh_kernel(groups, got, slow, new_slow, copies):
    total = sums = None
    for s in range(got.shape[0]):
        notes = wide(got[s, PIECE:])
        part = decoded(got[s, :PIECE], notes[0:1])
        total, sums = (part, notes) if s == 0 else (total + part, sums + notes)
    tok = sums[1:2]
    work = DIGIT * sums[2:3] + sums[3:4]
    everywhere = sums[4:5] + MIDDLE * got.shape[0]
    qsum = from_digits(sums[5:6], sums[6:7], sums[7:8])
    rate = outer_rate * groups * work / (tok * everywhere)
    place = own_place()
    for k in range(QUAD):

        @pl.when(place == k)
        def _(k=k):
            mine = own_parts(slow[0, 0], k)
            tile = mine[0] + rate * (total[:ROWS] - qsum * mine[0])
            rest = mine[1] + rate * (total[ROWS:] - qsum * mine[1])
            new_slow[0, 0] = own_block(tile, rest, k)
            for i in range(copies.shape[0]):
                copies[i, :ROWS] = tile.astype(BF16)
                copies[i, ROWS:] = rest.astype(BF16)


def lay_out_kernel(own, other, out):
    def body(pieces):
        group = lane_group((ROWS, LANES))
        for zh in range(own.shape[2]):
            at = zh * WIDE
            for k in range(QUAD):
                out[:, at + 2 * k * LANES : at + (2 * k + 1) * LANES] = pieces[k % 2][0, k // 2, zh, :ROWS]
            res = [unfolded(pieces[k % 2][0, k // 2, zh, ROWS:].astype(F32), k) for k in range(QUAD)]
            for k in range(QUAD - 1):
                odd = jnp.where(group < QUAD - 1 - k, res[k], res[k + 1])
                out[:, at + (2 * k + 1) * LANES : at + (2 * k + 2) * LANES] = odd.astype(BF16)

    for_core(lambda: body((own, other)), lambda: body((other, own)))


def call(kernel, out_shape, **more):
    return pl.pallas_call(
        kernel,
        out_shape=out_shape,
        compiler_params=pltpu.CompilerParams(vmem_limit_bytes=48 * 2**20),
        **more,
    )


def struct(shape, dtype):
    return jax.ShapeDtypeStruct(shape, dtype)


def swap(pieces, axis):
    return lax.all_to_all(pieces, axis, split_axis=0, concat_axis=0, tiled=True)


SCALAR = pl.BlockSpec(memory_space=pltpu.SMEM)
WHOLE = pl.BlockSpec(memory_space=pltpu.VMEM)


def shards(fast_weights, slow_weights, step_counts, token_counts):
    size = {a: lax.axis_size(a) for a in SHARD}
    groups = lax.axis_size("expert")
    nx, nzh = size["x"], size["zh"]
    fast = fast_weights[0, 0, 0]

    plane = nx * size["zl"]
    both = token_counts * FIELD + step_counts
    counts = swap(jnp.broadcast_to(both, (groups * size["c"], 1)), ("expert", "c"))
    other = lax.ppermute(fast, "c", [(0, 1), (1, 0)])
    shape = (nx, size["zl"], nzh, PIECE, LANES)
    keep = call(sort_kernel, struct(shape, BF16))(fast)
    pairs = call(
        pair_sum_kernel,
        struct((plane, nzh * PIECE + NOTES, LANES), jnp.int16),
        in_specs=[SCALAR, WHOLE, WHOLE],
    )(counts, keep, other)
    got = swap(pairs, ("x", "zl"))
    sums = call(near_sum_kernel, struct((nzh, PIECE + FAR_NOTES, LANES), jnp.int16))(got)
    got = swap(sums, "zh")
    new_slow, copies = call(
        lambda *refs: refresh_kernel(groups, *refs),
        (struct(slow_weights.shape, F32), struct((nzh, PIECE, LANES), BF16)),
    )(got, slow_weights)

    column = swap(copies, "zh")
    own = swap(jnp.broadcast_to(column[None], (plane, *column.shape)), ("x", "zl"))
    other = lax.ppermute(own, "c", [(0, 1), (1, 0)])
    cuts = 2
    planes = pl.BlockSpec((1, size["zl"], nzh // cuts, PIECE, LANES), lambda x, j: (x, 0, j, 0, 0))
    reset = call(
        lay_out_kernel,
        struct(fast.shape, BF16),
        grid=(nx, cuts),
        in_specs=[planes, planes],
        out_specs=pl.BlockSpec((ROWS, nzh // cuts * WIDE), lambda x, j: (0, cuts * x + j)),
    )(own.reshape(shape), other.reshape(shape))
    return new_slow, reset[None, None]


def solution(mesh):
    torus = Mesh(
        mesh.devices.reshape(mesh.shape["expert"], 2, 8, 2, 2),
        ("expert", *SHARD),
    )
    placed = (
        P("expert", SHARD, None, None, None),
        P("expert", None, None, SHARD),
        P("expert", SHARD),
        P("expert", SHARD),
    )
    return jax.shard_map(
        shards,
        mesh=torus,
        in_specs=placed,
        out_specs=(P("expert", None, None, SHARD), P("expert", None, None, None)),
        check_vma=False,
    )
```

```python
import jax
import jax.numpy as jnp
from jax import lax
from jax.experimental import pallas as pl
from jax.experimental.pallas import tpu as pltpu
from jax.sharding import Mesh
from jax.sharding import PartitionSpec as P

F32 = jnp.float32
BF16 = jnp.bfloat16

SHARD = ("x", "zh", "zl", "c")

outer_rate = 0.7

ROWS = 64
OWN = 224
LANES = 128
QUAD = 4
WIDE = QUAD * OWN
STEP = 32
TAIL = 16
REST = ROWS - TAIL

PIECE = ROWS + REST

NOTES = 16
FAR_NOTES = 8
FIELD = 2**16
PARTS = 8
TOP = 32767.0
DIGIT = 4096.0
MIDDLE = 32768.0
FINE = 8.0


def lane_group(shape):
    return lax.broadcasted_iota(jnp.int32, shape, 1) // STEP


def rolled(v, by):
    by %= LANES
    return jnp.concatenate([v[:, LANES - by :], v[:, : LANES - by]], axis=1) if by else v


def folded(res, k):
    free = QUAD - 1 - k
    tail = res[REST:]
    group = lane_group((TAIL, LANES))
    return jnp.concatenate(
        [jnp.where(group == free, rolled(tail, STEP * (m + 1)), res[m * TAIL : (m + 1) * TAIL]) for m in range(QUAD - 1)],
        axis=0,
    )


def unfolded(piece, k):
    free = QUAD - 1 - k
    group = lane_group((TAIL, LANES))
    tail = rolled(piece[:TAIL], -STEP)
    for m in range(1, QUAD - 1):
        moved = rolled(piece[m * TAIL : (m + 1) * TAIL], -STEP * (m + 1))
        tail = jnp.where(group == (free - m - 1) % QUAD, moved, tail)
    return jnp.concatenate([piece, tail], axis=0)


def own_parts(block, k):
    at = STEP * k
    res = [block[:, at + LANES :], jnp.zeros((ROWS, STEP), block.dtype), block[:, :at]]
    return block[:, at : at + LANES], folded(jnp.concatenate([r for r in res if r.shape[1]], axis=1), k)


def own_block(tile, piece, k):
    at = STEP * k
    res = unfolded(piece, k)
    parts = [res[:, LANES - at :] if k else res[:, :0], tile, res[:, : LANES - STEP - at]]
    return jnp.concatenate([p for p in parts if p.shape[1]], axis=1)


def own_place():
    return lax.axis_index("zl") * 2 + lax.axis_index("c")


def for_core(first, second):
    core = lax.axis_index("c")
    pl.when(core == 0)(first)
    pl.when(core != 0)(second)


def in_rows(values, rows):
    row = lax.broadcasted_iota(jnp.int32, (rows, LANES), 0)
    out = jnp.zeros((rows, LANES), F32)
    for i, value in enumerate(values):
        out = jnp.where(row == i, value, out)
    return out


def digits(value):
    whole = jnp.floor(value)
    part = (value - whole) * DIGIT
    digit = jnp.floor(part)
    return whole, digit, jnp.floor((part - digit) * DIGIT)


def from_digits(whole, first, second):
    return whole + (first + second * (1 / DIGIT)) * (1 / DIGIT)


def coded(total):
    largest = jnp.maximum(jnp.max(jnp.abs(total), axis=0, keepdims=True), 1e-30)
    level = jnp.ceil(FINE * jnp.log2(largest))
    units = jnp.clip(jnp.round(total * (TOP * jnp.exp2(level * (-1 / FINE)))), -TOP, TOP)
    return short(units), level


def short(values):
    return values.astype(jnp.int32).astype(jnp.int16)


def wide(values):
    return values.astype(jnp.int32).astype(F32)


def decoded(units, level):
    return (jnp.exp2(level * (1 / FINE)) * (1 / TOP)) * wide(units)


def fields(both):
    return both // FIELD, both % FIELD


def own_pieces(fast, g, core):
    group = lane_group((ROWS, LANES))
    lanes = [slice(g * WIDE + i * LANES, g * WIDE + (i + 1) * LANES) for i in range(2 * QUAD - 1)]
    odd = [fast[:, at].astype(F32) for at in lanes[1::2]]
    pieces = []
    for k in range(core, QUAD, 2):
        if k == 0:
            res = odd[0]
        elif k == QUAD - 1:
            res = odd[-1]
        else:
            res = jnp.where(group >= QUAD - k, odd[k - 1], odd[k])
        pieces.append((fast[:, lanes[2 * k]].astype(F32), folded(res, k)))
    return pieces


def sort_kernel(fast, keep):
    nx, n_zl, n_zh = keep.shape[:3]

    def body(core):
        for g in range(nx * n_zh):
            x, zh = divmod(g, n_zh)
            for zl, (tile, rest) in enumerate(own_pieces(fast, g, core)):
                keep[x, zl, zh, :ROWS] = tile.astype(BF16)
                keep[x, zl, zh, ROWS:] = rest.astype(BF16)

    for_core(lambda: body(0), lambda: body(1))


def pair_sum_kernel(counts, keep, other, out):
    nx, n_zl, n_zh = keep.shape[:3]

    def body(core):
        pair = lax.axis_index("expert") * 2
        both = [counts[pair + c, 0] for c in (core, 1 - core)]
        tokens, steps = ([jnp.full((1, LANES), v.astype(F32)) for v in f] for f in zip(*map(fields, both)))
        shares = [t / n for t, n in zip(tokens, steps)]
        everywhere = sum(fields(counts[i, 0])[0] for i in range(counts.shape[0])).astype(F32)
        work = sum(t * n for t, n in zip(tokens, steps))
        sums = (sum(tokens), work, *digits(sum(shares)), everywhere)
        levels = [[] for _ in range(out.shape[0])]
        for g in range(nx * n_zh):
            x, zh = divmod(g, n_zh)
            for zl, parts in enumerate(own_pieces(other, g, core)):
                d = x * n_zl + zl
                mix = shares[0] * keep[x, zl, zh].astype(F32) + shares[1] * jnp.concatenate(parts, axis=0)
                out[d, zh * PIECE : (zh + 1) * PIECE], level = coded(mix)
                levels[d].append(level)
        for d in range(out.shape[0]):
            out[d, n_zh * PIECE :] = short(in_rows((*levels[d], *sums), NOTES))

    for_core(lambda: body(0), lambda: body(1))


def near_sum_kernel(got, out):
    n, n_zh = got.shape[0], out.shape[0]
    notes = [wide(got[s, n_zh * PIECE :]) for s in range(n)]
    tok, work, *qsum, everywhere = (sum(v[n_zh + i : n_zh + i + 1] for v in notes) for i in range(6))
    high = jnp.floor(work / DIGIT)
    far = (tok, high, work - DIGIT * high, everywhere - MIDDLE, *digits(from_digits(*qsum)))
    for zh in range(n_zh):
        piece = slice(zh * PIECE, (zh + 1) * PIECE)
        total = decoded(got[0, piece], notes[0][zh : zh + 1])
        for s in range(1, n):
            total = total + decoded(got[s, piece], notes[s][zh : zh + 1])
        out[zh, :PIECE], level = coded(total)
        out[zh, PIECE:] = short(in_rows((level, *far), FAR_NOTES))


def refresh_kernel(groups, got, slow, new_slow, copies):
    total = sums = None
    for s in range(got.shape[0]):
        notes = wide(got[s, PIECE:])
        part = decoded(got[s, :PIECE], notes[0:1])
        total, sums = (part, notes) if s == 0 else (total + part, sums + notes)
    tok = sums[1:2]
    work = DIGIT * sums[2:3] + sums[3:4]
    everywhere = sums[4:5] + MIDDLE * got.shape[0]
    qsum = from_digits(sums[5:6], sums[6:7], sums[7:8])
    rate = outer_rate * groups * work / (tok * everywhere)
    place = own_place()
    for k in range(QUAD):

        @pl.when(place == k)
        def _(k=k):
            mine = own_parts(slow[0, 0], k)
            tile = mine[0] + rate * (total[:ROWS] - qsum * mine[0])
            rest = mine[1] + rate * (total[ROWS:] - qsum * mine[1])
            new_slow[0, 0] = own_block(tile, rest, k)
            for i in range(copies.shape[0]):
                copies[i, :ROWS] = tile.astype(BF16)
                copies[i, ROWS:] = rest.astype(BF16)


def lay_out_kernel(own, other, out, whole, sems):
    n_zh = own.shape[2]
    part = whole.shape[1] // sems.shape[0]

    def body(pieces):
        group = lane_group((ROWS, LANES))
        stores = []
        for g in range(whole.shape[1] // WIDE):
            x, zh = divmod(g, n_zh)
            at = g * WIDE
            for k in range(QUAD):
                whole[:, at + 2 * k * LANES : at + (2 * k + 1) * LANES] = pieces[k % 2][x, k // 2, zh, :ROWS]
            res = [unfolded(pieces[k % 2][x, k // 2, zh, ROWS:].astype(F32), k) for k in range(QUAD)]
            for k in range(QUAD - 1):
                odd = jnp.where(group < QUAD - 1 - k, res[k], res[k + 1])
                whole[:, at + (2 * k + 1) * LANES : at + (2 * k + 2) * LANES] = odd.astype(BF16)
            if (at + WIDE) % part == 0:
                i = at // part
                span = pl.ds(i * part, part)
                stores.append(pltpu.make_async_copy(whole.at[:, span], out.at[:, span], sems.at[i]))
                stores[-1].start()
        for store in stores:
            store.wait()

    for_core(lambda: body((own, other)), lambda: body((other, own)))


def call(kernel, out_shape, **more):
    return pl.pallas_call(
        kernel,
        out_shape=out_shape,
        compiler_params=pltpu.CompilerParams(vmem_limit_bytes=48 * 2**20),
        **more,
    )


def struct(shape, dtype):
    return jax.ShapeDtypeStruct(shape, dtype)


def swap(pieces, axis):
    return lax.all_to_all(pieces, axis, split_axis=0, concat_axis=0, tiled=True)


SCALAR = pl.BlockSpec(memory_space=pltpu.SMEM)
WHOLE = pl.BlockSpec(memory_space=pltpu.VMEM)


def shards(fast_weights, slow_weights, step_counts, token_counts):
    size = {a: lax.axis_size(a) for a in SHARD}
    groups = lax.axis_size("expert")
    nx, nzh = size["x"], size["zh"]
    fast = fast_weights[0, 0, 0]

    plane = nx * size["zl"]
    both = token_counts * FIELD + step_counts
    counts = swap(jnp.broadcast_to(both, (groups * size["c"], 1)), ("expert", "c"))
    other = lax.ppermute(fast, "c", [(0, 1), (1, 0)])
    shape = (nx, size["zl"], nzh, PIECE, LANES)
    keep = call(sort_kernel, struct(shape, BF16))(fast)
    pairs = call(
        pair_sum_kernel,
        struct((plane, nzh * PIECE + NOTES, LANES), jnp.int16),
        in_specs=[SCALAR, WHOLE, WHOLE],
    )(counts, keep, other)
    got = swap(pairs, ("x", "zl"))
    sums = call(near_sum_kernel, struct((nzh, PIECE + FAR_NOTES, LANES), jnp.int16))(got)
    got = swap(sums, "zh")
    new_slow, copies = call(
        lambda *refs: refresh_kernel(groups, *refs),
        (struct(slow_weights.shape, F32), struct((nzh, PIECE, LANES), BF16)),
    )(got, slow_weights)

    column = swap(copies, "zh")
    own = swap(jnp.broadcast_to(column[None], (plane, *column.shape)), ("x", "zl"))
    other = lax.ppermute(own, "c", [(0, 1), (1, 0)])
    reset = call(
        lay_out_kernel,
        struct(fast.shape, BF16),
        out_specs=pl.BlockSpec(memory_space=pltpu.HBM),
        scratch_shapes=[pltpu.VMEM(fast.shape, BF16), pltpu.SemaphoreType.DMA((PARTS,))],
    )(own.reshape(shape), other.reshape(shape))
    return new_slow, reset[None, None]


def solution(mesh):
    torus = Mesh(
        mesh.devices.reshape(mesh.shape["expert"], 2, 8, 2, 2),
        ("expert", *SHARD),
    )
    placed = (
        P("expert", SHARD, None, None, None),
        P("expert", None, None, SHARD),
        P("expert", SHARD),
        P("expert", SHARD),
    )
    return jax.shard_map(
        shards,
        mesh=torus,
        in_specs=placed,
        out_specs=(P("expert", None, None, SHARD), P("expert", None, None, None)),
        check_vma=False,
    )
```

```python
import jax
import jax.numpy as jnp
from jax import lax
from jax.experimental import pallas as pl
from jax.experimental.pallas import tpu as pltpu
from jax.sharding import Mesh
from jax.sharding import PartitionSpec as P

F32 = jnp.float32
BF16 = jnp.bfloat16

SHARD = ("x", "zh", "zl", "c")

outer_rate = 0.7

ROWS = 64
OWN = 224
LANES = 128
QUAD = 4
WIDE = QUAD * OWN
STEP = 32
TAIL = 16
REST = ROWS - TAIL

PIECE = ROWS + REST

NOTES = 16
FAR_NOTES = 8
FIELD = 2**16
PARTS = 8
TOP = 32767.0
DIGIT = 4096.0
MIDDLE = 32768.0
FINE = 8.0


def lane_group(shape):
    return lax.broadcasted_iota(jnp.int32, shape, 1) // STEP


def rolled(v, by):
    by %= LANES
    return jnp.concatenate([v[:, LANES - by :], v[:, : LANES - by]], axis=1) if by else v


def folded(res, k):
    free = QUAD - 1 - k
    tail = res[REST:]
    group = lane_group((TAIL, LANES))
    return jnp.concatenate(
        [jnp.where(group == free, rolled(tail, STEP * (m + 1)), res[m * TAIL : (m + 1) * TAIL]) for m in range(QUAD - 1)],
        axis=0,
    )


def unfolded(piece, k):
    free = QUAD - 1 - k
    group = lane_group((TAIL, LANES))
    tail = rolled(piece[:TAIL], -STEP)
    for m in range(1, QUAD - 1):
        moved = rolled(piece[m * TAIL : (m + 1) * TAIL], -STEP * (m + 1))
        tail = jnp.where(group == (free - m - 1) % QUAD, moved, tail)
    return jnp.concatenate([piece, tail], axis=0)


def own_parts(block, k):
    at = STEP * k
    res = [block[:, at + LANES :], jnp.zeros((ROWS, STEP), block.dtype), block[:, :at]]
    return block[:, at : at + LANES], folded(jnp.concatenate([r for r in res if r.shape[1]], axis=1), k)


def own_block(tile, piece, k):
    at = STEP * k
    res = unfolded(piece, k)
    parts = [res[:, LANES - at :] if k else res[:, :0], tile, res[:, : LANES - STEP - at]]
    return jnp.concatenate([p for p in parts if p.shape[1]], axis=1)


def own_place():
    return lax.axis_index("zl") * 2 + lax.axis_index("c")


def for_core(first, second):
    core = lax.axis_index("c")
    pl.when(core == 0)(first)
    pl.when(core != 0)(second)


def in_rows(values, rows):
    row = lax.broadcasted_iota(jnp.int32, (rows, LANES), 0)
    out = jnp.zeros((rows, LANES), F32)
    for i, value in enumerate(values):
        out = jnp.where(row == i, value, out)
    return out


def digits(value):
    whole = jnp.floor(value)
    part = (value - whole) * DIGIT
    digit = jnp.floor(part)
    return whole, digit, jnp.floor((part - digit) * DIGIT)


def from_digits(whole, first, second):
    return whole + (first + second * (1 / DIGIT)) * (1 / DIGIT)


def coded(total):
    largest = jnp.maximum(jnp.max(jnp.abs(total), axis=0, keepdims=True), 1e-30)
    level = jnp.ceil(FINE * jnp.log2(largest))
    units = jnp.clip(jnp.round(total * (TOP * jnp.exp2(level * (-1 / FINE)))), -TOP, TOP)
    return short(units), level


def short(values):
    return values.astype(jnp.int32).astype(jnp.int16)


def wide(values):
    return values.astype(jnp.int32).astype(F32)


def decoded(units, level):
    return (jnp.exp2(level * (1 / FINE)) * (1 / TOP)) * wide(units)


def fields(both):
    return both // FIELD, both % FIELD


def own_pieces(fast, g, core):
    group = lane_group((ROWS, LANES))
    lanes = [slice(g * WIDE + i * LANES, g * WIDE + (i + 1) * LANES) for i in range(2 * QUAD - 1)]
    odd = [fast[:, at].astype(F32) for at in lanes[1::2]]
    pieces = []
    for k in range(core, QUAD, 2):
        if k == 0:
            res = odd[0]
        elif k == QUAD - 1:
            res = odd[-1]
        else:
            res = jnp.where(group >= QUAD - k, odd[k - 1], odd[k])
        pieces.append((fast[:, lanes[2 * k]].astype(F32), folded(res, k)))
    return pieces


def for_own_place(body):
    place = own_place()
    for k in range(QUAD):
        pl.when(place == k)(lambda k=k: body(k))


def sort_kernel(fast, slow, keep, mine):
    nx, n_zl, n_zh = keep.shape[:3]

    def pack(k):
        mine[:ROWS], mine[ROWS:] = own_parts(slow[0, 0], k)

    for_own_place(pack)

    def body(core):
        for g in range(nx * n_zh):
            x, zh = divmod(g, n_zh)
            for zl, (tile, rest) in enumerate(own_pieces(fast, g, core)):
                keep[x, zl, zh, :ROWS] = tile.astype(BF16)
                keep[x, zl, zh, ROWS:] = rest.astype(BF16)

    for_core(lambda: body(0), lambda: body(1))


def pair_sum_kernel(counts, keep, other, out):
    nx, n_zl, n_zh = keep.shape[:3]

    def body(core):
        pair = lax.axis_index("expert") * 2
        both = [counts[pair + c, 0] for c in (core, 1 - core)]
        tokens, steps = ([jnp.full((1, LANES), v.astype(F32)) for v in f] for f in zip(*map(fields, both)))
        shares = [t / n for t, n in zip(tokens, steps)]
        everywhere = sum(fields(counts[i, 0])[0] for i in range(counts.shape[0])).astype(F32)
        work = sum(t * n for t, n in zip(tokens, steps))
        sums = (sum(tokens), work, *digits(sum(shares)), everywhere)
        levels = [[] for _ in range(out.shape[0])]
        for g in range(nx * n_zh):
            x, zh = divmod(g, n_zh)
            for zl, parts in enumerate(own_pieces(other, g, core)):
                d = x * n_zl + zl
                mix = shares[0] * keep[x, zl, zh].astype(F32) + shares[1] * jnp.concatenate(parts, axis=0)
                out[d, zh * PIECE : (zh + 1) * PIECE], level = coded(mix)
                levels[d].append(level)
        for d in range(out.shape[0]):
            out[d, n_zh * PIECE :] = short(in_rows((*levels[d], *sums), NOTES))

    for_core(lambda: body(0), lambda: body(1))


def near_sum_kernel(got, out):
    n, n_zh = got.shape[0], out.shape[0]
    notes = [wide(got[s, n_zh * PIECE :]) for s in range(n)]
    tok, work, *qsum, everywhere = (sum(v[n_zh + i : n_zh + i + 1] for v in notes) for i in range(6))
    high = jnp.floor(work / DIGIT)
    far = (tok, high, work - DIGIT * high, everywhere - MIDDLE, *digits(from_digits(*qsum)))
    for zh in range(n_zh):
        piece = slice(zh * PIECE, (zh + 1) * PIECE)
        total = decoded(got[0, piece], notes[0][zh : zh + 1])
        for s in range(1, n):
            total = total + decoded(got[s, piece], notes[s][zh : zh + 1])
        out[zh, :PIECE], level = coded(total)
        out[zh, PIECE:] = short(in_rows((level, *far), FAR_NOTES))


def refresh_kernel(groups, got, mine, fresh, copies):
    total = sums = None
    for s in range(got.shape[0]):
        notes = wide(got[s, PIECE:])
        part = decoded(got[s, :PIECE], notes[0:1])
        total, sums = (part, notes) if s == 0 else (total + part, sums + notes)
    tok = sums[1:2]
    work = DIGIT * sums[2:3] + sums[3:4]
    everywhere = sums[4:5] + MIDDLE * got.shape[0]
    qsum = from_digits(sums[5:6], sums[6:7], sums[7:8])
    rate = outer_rate * groups * work / (tok * everywhere)
    new = mine[...] + rate * (total - qsum * mine[...])
    fresh[...] = new
    for i in range(copies.shape[0]):
        copies[i] = new.astype(BF16)


def side_kernel(fresh, own, new_slow, half):
    def unpack(k):
        new_slow[0, 0] = own_block(fresh[:ROWS], fresh[ROWS:], k)

    for_own_place(unpack)

    def body(core):
        for at, k, piece in pieces_of(own, core):
            half[:, at + 2 * k * LANES : at + (2 * k + 1) * LANES] = piece[:ROWS]
            res = unfolded(piece[ROWS:].astype(F32), k).astype(BF16)
            for i in beside(k):
                half[:, at + i * LANES : at + (i + 1) * LANES] = res

    for_core(lambda: body(0), lambda: body(1))


def pieces_of(pieces, core):
    for g in range(pieces.shape[0] * pieces.shape[2]):
        x, zh = divmod(g, pieces.shape[2])
        for zl in range(pieces.shape[1]):
            yield g * WIDE, 2 * zl + core, pieces[x, zl, zh]


def beside(k):
    return [i for i in (2 * k - 1, 2 * k + 1) if 0 < i < 2 * QUAD - 1]


def lay_out_kernel(half, other, out, whole, sems):
    part = whole.shape[1] // sems.shape[0]
    group = lane_group((ROWS, LANES))

    def body(core):
        stores = []
        for at, k, piece in pieces_of(other, 1 - core):
            mine = at + 2 * (k + 2 * core - 1) * LANES
            whole[:, mine : mine + LANES] = half[:, mine : mine + LANES]
            whole[:, at + 2 * k * LANES : at + (2 * k + 1) * LANES] = piece[:ROWS]
            res = unfolded(piece[ROWS:].astype(F32), k)
            for i in beside(k):
                span = slice(at + i * LANES, at + (i + 1) * LANES)
                left = group < QUAD - 1 - i // 2
                theirs = left if i > 2 * k else jnp.logical_not(left)
                whole[:, span] = jnp.where(theirs, res, half[:, span].astype(F32)).astype(BF16)
            if k // 2 == 1 and (at + WIDE) % part == 0:
                i = at // part
                span = pl.ds(i * part, part)
                stores.append(pltpu.make_async_copy(whole.at[:, span], out.at[:, span], sems.at[i]))
                stores[-1].start()
        for store in stores:
            store.wait()

    for_core(lambda: body(0), lambda: body(1))


def call(kernel, out_shape, **more):
    return pl.pallas_call(
        kernel,
        out_shape=out_shape,
        compiler_params=pltpu.CompilerParams(vmem_limit_bytes=48 * 2**20),
        **more,
    )


def struct(shape, dtype):
    return jax.ShapeDtypeStruct(shape, dtype)


def swap(pieces, axis):
    return lax.all_to_all(pieces, axis, split_axis=0, concat_axis=0, tiled=True)


SCALAR = pl.BlockSpec(memory_space=pltpu.SMEM)
WHOLE = pl.BlockSpec(memory_space=pltpu.VMEM)


def shards(fast_weights, slow_weights, step_counts, token_counts):
    size = {a: lax.axis_size(a) for a in SHARD}
    groups = lax.axis_size("expert")
    nx, nzh = size["x"], size["zh"]
    fast = fast_weights[0, 0, 0]

    plane = nx * size["zl"]
    both = token_counts * FIELD + step_counts
    counts = swap(jnp.broadcast_to(both, (groups * size["c"], 1)), ("expert", "c"))
    other = lax.ppermute(fast, "c", [(0, 1), (1, 0)])
    shape = (nx, size["zl"], nzh, PIECE, LANES)
    block = struct((PIECE, LANES), F32)
    keep, mine = call(sort_kernel, (struct(shape, BF16), block))(fast, slow_weights)
    pairs = call(
        pair_sum_kernel,
        struct((plane, nzh * PIECE + NOTES, LANES), jnp.int16),
        in_specs=[SCALAR, WHOLE, WHOLE],
    )(counts, keep, other)
    got = swap(pairs, ("x", "zl"))
    sums = call(near_sum_kernel, struct((nzh, PIECE + FAR_NOTES, LANES), jnp.int16))(got)
    got = swap(sums, "zh")
    fresh, copies = call(
        lambda *refs: refresh_kernel(groups, *refs), (block, struct((nzh, PIECE, LANES), BF16))
    )(got, mine)

    column = swap(copies, "zh")
    own = swap(jnp.broadcast_to(column[None], (plane, *column.shape)), ("x", "zl"))
    other = lax.ppermute(own, "c", [(0, 1), (1, 0)])
    new_slow, half = call(side_kernel, (struct(slow_weights.shape, F32), struct(fast.shape, BF16)))(
        fresh, own.reshape(shape)
    )
    reset = call(
        lay_out_kernel,
        struct(fast.shape, BF16),
        out_specs=pl.BlockSpec(memory_space=pltpu.HBM),
        scratch_shapes=[pltpu.VMEM(fast.shape, BF16), pltpu.SemaphoreType.DMA((PARTS,))],
    )(half, other.reshape(shape))
    return new_slow, reset[None, None]


def solution(mesh):
    torus = Mesh(
        mesh.devices.reshape(mesh.shape["expert"], 2, 8, 2, 2),
        ("expert", *SHARD),
    )
    placed = (
        P("expert", SHARD, None, None, None),
        P("expert", None, None, SHARD),
        P("expert", SHARD),
        P("expert", SHARD),
    )
    return jax.shard_map(
        shards,
        mesh=torus,
        in_specs=placed,
        out_specs=(P("expert", None, None, SHARD), P("expert", None, None, None)),
        check_vma=False,
    )
```

```python
import jax
import jax.numpy as jnp
from jax import lax
from jax.experimental import pallas as pl
from jax.experimental.pallas import tpu as pltpu
from jax.sharding import Mesh
from jax.sharding import PartitionSpec as P

F32 = jnp.float32
BF16 = jnp.bfloat16

SHARD = ("x", "zh", "zl", "c")

outer_rate = 0.7

ROWS = 64
OWN = 224
LANES = 128
QUAD = 4
WIDE = QUAD * OWN
STEP = 32
TAIL = 16
REST = ROWS - TAIL

PIECE = ROWS + REST

NOTES = 16
FAR_NOTES = 8
FIELD = 2**16
PARTS = 8
TOP = 32767.0
DIGIT = 4096.0
MIDDLE = 32768.0
FINE = 8.0


def lane_group(shape):
    return lax.broadcasted_iota(jnp.int32, shape, 1) // STEP


def rolled(v, by):
    return pltpu.roll(v, by % LANES, 1)


def folded(res, k):
    free = QUAD - 1 - k
    tail = res[REST:]
    group = lane_group((TAIL, LANES))
    return jnp.concatenate(
        [jnp.where(group == free, rolled(tail, STEP * (m + 1)), res[m * TAIL : (m + 1) * TAIL]) for m in range(QUAD - 1)],
        axis=0,
    )


def unfolded(piece, k):
    free = QUAD - 1 - k
    group = lane_group((TAIL, LANES))
    tail = rolled(piece[:TAIL], -STEP)
    for m in range(1, QUAD - 1):
        moved = rolled(piece[m * TAIL : (m + 1) * TAIL], -STEP * (m + 1))
        tail = jnp.where(group == (free - m - 1) % QUAD, moved, tail)
    return jnp.concatenate([piece, tail], axis=0)


def own_parts(block, k):
    at = STEP * k
    res = [block[:, at + LANES :], jnp.zeros((ROWS, STEP), block.dtype), block[:, :at]]
    return block[:, at : at + LANES], folded(jnp.concatenate([r for r in res if r.shape[1]], axis=1), k)


def own_block(tile, piece, k):
    at = STEP * k
    res = unfolded(piece, k)
    parts = [res[:, LANES - at :] if k else res[:, :0], tile, res[:, : LANES - STEP - at]]
    return jnp.concatenate([p for p in parts if p.shape[1]], axis=1)


def own_place():
    return lax.axis_index("zl") * 2 + lax.axis_index("c")


def for_core(first, second):
    core = lax.axis_index("c")
    pl.when(core == 0)(first)
    pl.when(core != 0)(second)


def in_rows(values, rows):
    row = lax.broadcasted_iota(jnp.int32, (rows, LANES), 0)
    out = jnp.zeros((rows, LANES), F32)
    for i, value in enumerate(values):
        out = jnp.where(row == i, value, out)
    return out


def digits(value):
    whole = jnp.floor(value)
    part = (value - whole) * DIGIT
    digit = jnp.floor(part)
    return whole, digit, jnp.floor((part - digit) * DIGIT)


def from_digits(whole, first, second):
    return whole + (first + second * (1 / DIGIT)) * (1 / DIGIT)


def coded(total):
    largest = jnp.maximum(jnp.max(jnp.abs(total), axis=0, keepdims=True), 1e-30)
    level = jnp.ceil(FINE * jnp.log2(largest))
    units = jnp.clip(jnp.round(total * (TOP * jnp.exp2(level * (-1 / FINE)))), -TOP, TOP)
    return short(units), level


def short(values):
    return values.astype(jnp.int32).astype(jnp.int16)


def wide(values):
    return values.astype(jnp.int32).astype(F32)


def decoded(units, level):
    return (jnp.exp2(level * (1 / FINE)) * (1 / TOP)) * wide(units)


def fields(both):
    return both // FIELD, both % FIELD


def own_pieces(fast, g, core):
    group = lane_group((ROWS, LANES))
    lanes = [slice(g * WIDE + i * LANES, g * WIDE + (i + 1) * LANES) for i in range(2 * QUAD - 1)]
    odd = [fast[:, at].astype(F32) for at in lanes[1::2]]
    pieces = []
    for k in range(core, QUAD, 2):
        if k == 0:
            res = odd[0]
        elif k == QUAD - 1:
            res = odd[-1]
        else:
            res = jnp.where(group >= QUAD - k, odd[k - 1], odd[k])
        pieces.append((fast[:, lanes[2 * k]].astype(F32), folded(res, k)))
    return pieces


def for_own_place(body):
    place = own_place()
    for k in range(QUAD):
        pl.when(place == k)(lambda k=k: body(k))


def sort_kernel(fast, slow, keep, mine):
    nx, n_zl, n_zh = keep.shape[:3]

    def pack(k):
        mine[:ROWS], mine[ROWS:] = own_parts(slow[0, 0], k)

    for_own_place(pack)

    def body(core):
        for g in range(nx * n_zh):
            x, zh = divmod(g, n_zh)
            for zl, (tile, rest) in enumerate(own_pieces(fast, g, core)):
                keep[x, zl, zh, :ROWS] = tile.astype(BF16)
                keep[x, zl, zh, ROWS:] = rest.astype(BF16)

    for_core(lambda: body(0), lambda: body(1))


def pair_sum_kernel(counts, keep, other, out):
    nx, n_zl, n_zh = keep.shape[:3]

    def body(core):
        pair = lax.axis_index("expert") * 2
        both = [counts[pair + c, 0] for c in (core, 1 - core)]
        tokens, steps = ([jnp.full((1, LANES), v.astype(F32)) for v in f] for f in zip(*map(fields, both)))
        shares = [t / n for t, n in zip(tokens, steps)]
        everywhere = sum(fields(counts[i, 0])[0] for i in range(counts.shape[0])).astype(F32)
        work = sum(t * n for t, n in zip(tokens, steps))
        sums = (sum(tokens), work, *digits(sum(shares)), everywhere)
        levels = [[] for _ in range(out.shape[0])]
        for g in range(nx * n_zh):
            x, zh = divmod(g, n_zh)
            for zl, parts in enumerate(own_pieces(other, g, core)):
                d = x * n_zl + zl
                mix = shares[0] * keep[x, zl, zh].astype(F32) + shares[1] * jnp.concatenate(parts, axis=0)
                out[d, zh * PIECE : (zh + 1) * PIECE], level = coded(mix)
                levels[d].append(level)
        for d in range(out.shape[0]):
            out[d, n_zh * PIECE :] = short(in_rows((*levels[d], *sums), NOTES))

    for_core(lambda: body(0), lambda: body(1))


def near_sum_kernel(got, out):
    n, n_zh = got.shape[0], out.shape[0]
    notes = [wide(got[s, n_zh * PIECE :]) for s in range(n)]
    tok, work, *qsum, everywhere = (sum(v[n_zh + i : n_zh + i + 1] for v in notes) for i in range(6))
    high = jnp.floor(work / DIGIT)
    far = (tok, high, work - DIGIT * high, everywhere - MIDDLE, *digits(from_digits(*qsum)))
    for zh in range(n_zh):
        piece = slice(zh * PIECE, (zh + 1) * PIECE)
        total = decoded(got[0, piece], notes[0][zh : zh + 1])
        for s in range(1, n):
            total = total + decoded(got[s, piece], notes[s][zh : zh + 1])
        out[zh, :PIECE], level = coded(total)
        out[zh, PIECE:] = short(in_rows((level, *far), FAR_NOTES))


def refresh_kernel(groups, got, mine, fresh, copies):
    total = sums = None
    for s in range(got.shape[0]):
        notes = wide(got[s, PIECE:])
        part = decoded(got[s, :PIECE], notes[0:1])
        total, sums = (part, notes) if s == 0 else (total + part, sums + notes)
    tok = sums[1:2]
    work = DIGIT * sums[2:3] + sums[3:4]
    everywhere = sums[4:5] + MIDDLE * got.shape[0]
    qsum = from_digits(sums[5:6], sums[6:7], sums[7:8])
    rate = outer_rate * groups * work / (tok * everywhere)
    new = mine[...] + rate * (total - qsum * mine[...])
    fresh[...] = new
    for i in range(copies.shape[0]):
        copies[i] = new.astype(BF16)


def side_kernel(fresh, own, new_slow, half):
    def unpack(k):
        new_slow[0, 0] = own_block(fresh[:ROWS], fresh[ROWS:], k)

    for_own_place(unpack)

    def body(core):
        for at, k, piece in pieces_of(own, core):
            half[:, at + 2 * k * LANES : at + (2 * k + 1) * LANES] = piece[:ROWS]
            res = unfolded(piece[ROWS:].astype(F32), k).astype(BF16)
            for i in beside(k):
                half[:, at + i * LANES : at + (i + 1) * LANES] = res

    for_core(lambda: body(0), lambda: body(1))


def pieces_of(pieces, core):
    for g in range(pieces.shape[0] * pieces.shape[2]):
        x, zh = divmod(g, pieces.shape[2])
        for zl in range(pieces.shape[1]):
            yield g * WIDE, 2 * zl + core, pieces[x, zl, zh]


def beside(k):
    return [i for i in (2 * k - 1, 2 * k + 1) if 0 < i < 2 * QUAD - 1]


def lay_out_kernel(half, other, out, whole, sems):
    part = whole.shape[1] // sems.shape[0]
    group = lane_group((ROWS, LANES))

    def body(core):
        stores = []
        for at, k, piece in pieces_of(other, 1 - core):
            mine = at + 2 * (k + 2 * core - 1) * LANES
            whole[:, mine : mine + LANES] = half[:, mine : mine + LANES]
            whole[:, at + 2 * k * LANES : at + (2 * k + 1) * LANES] = piece[:ROWS]
            res = unfolded(piece[ROWS:].astype(F32), k)
            for i in beside(k):
                span = slice(at + i * LANES, at + (i + 1) * LANES)
                left = group < QUAD - 1 - i // 2
                theirs = left if i > 2 * k else jnp.logical_not(left)
                whole[:, span] = jnp.where(theirs, res, half[:, span].astype(F32)).astype(BF16)
            if k // 2 == 1 and (at + WIDE) % part == 0:
                i = at // part
                span = pl.ds(i * part, part)
                stores.append(pltpu.make_async_copy(whole.at[:, span], out.at[:, span], sems.at[i]))
                stores[-1].start()
        for store in stores:
            store.wait()

    for_core(lambda: body(0), lambda: body(1))


def call(kernel, out_shape, **more):
    return pl.pallas_call(
        kernel,
        out_shape=out_shape,
        compiler_params=pltpu.CompilerParams(vmem_limit_bytes=48 * 2**20),
        **more,
    )


def struct(shape, dtype):
    return jax.ShapeDtypeStruct(shape, dtype)


def swap(pieces, axis):
    return lax.all_to_all(pieces, axis, split_axis=0, concat_axis=0, tiled=True)


SCALAR = pl.BlockSpec(memory_space=pltpu.SMEM)
WHOLE = pl.BlockSpec(memory_space=pltpu.VMEM)


def shards(fast_weights, slow_weights, step_counts, token_counts):
    size = {a: lax.axis_size(a) for a in SHARD}
    groups = lax.axis_size("expert")
    nx, nzh = size["x"], size["zh"]
    fast = fast_weights[0, 0, 0]

    plane = nx * size["zl"]
    both = token_counts * FIELD + step_counts
    counts = swap(jnp.broadcast_to(both, (groups * size["c"], 1)), ("expert", "c"))
    other = lax.ppermute(fast, "c", [(0, 1), (1, 0)])
    shape = (nx, size["zl"], nzh, PIECE, LANES)
    block = struct((PIECE, LANES), F32)
    keep, mine = call(sort_kernel, (struct(shape, BF16), block))(fast, slow_weights)
    pairs = call(
        pair_sum_kernel,
        struct((plane, nzh * PIECE + NOTES, LANES), jnp.int16),
        in_specs=[SCALAR, WHOLE, WHOLE],
    )(counts, keep, other)
    got = swap(pairs, ("x", "zl"))
    sums = call(near_sum_kernel, struct((nzh, PIECE + FAR_NOTES, LANES), jnp.int16))(got)
    got = swap(sums, "zh")
    fresh, copies = call(
        lambda *refs: refresh_kernel(groups, *refs), (block, struct((nzh, PIECE, LANES), BF16))
    )(got, mine)

    column = swap(copies, "zh")
    own = swap(jnp.broadcast_to(column[None], (plane, *column.shape)), ("x", "zl"))
    other = lax.ppermute(own, "c", [(0, 1), (1, 0)])
    new_slow, half = call(side_kernel, (struct(slow_weights.shape, F32), struct(fast.shape, BF16)))(
        fresh, own.reshape(shape)
    )
    reset = call(
        lay_out_kernel,
        struct(fast.shape, BF16),
        out_specs=pl.BlockSpec(memory_space=pltpu.HBM),
        scratch_shapes=[pltpu.VMEM(fast.shape, BF16), pltpu.SemaphoreType.DMA((PARTS,))],
    )(half, other.reshape(shape))
    return new_slow, reset[None, None]


def solution(mesh):
    torus = Mesh(
        mesh.devices.reshape(mesh.shape["expert"], 2, 8, 2, 2),
        ("expert", *SHARD),
    )
    placed = (
        P("expert", SHARD, None, None, None),
        P("expert", None, None, SHARD),
        P("expert", SHARD),
        P("expert", SHARD),
    )
    return jax.shard_map(
        shards,
        mesh=torus,
        in_specs=placed,
        out_specs=(P("expert", None, None, SHARD), P("expert", None, None, None)),
        check_vma=False,
    )
```

```python
import jax
import jax.numpy as jnp
from jax import lax
from jax.experimental import pallas as pl
from jax.experimental.pallas import tpu as pltpu
from jax.sharding import Mesh
from jax.sharding import PartitionSpec as P

F32 = jnp.float32
BF16 = jnp.bfloat16

SHARD = ("x", "zh", "zl", "c")

outer_rate = 0.7

ROWS = 64
OWN = 224
LANES = 128
QUAD = 4
WIDE = QUAD * OWN
STEP = 32
TAIL = 16
REST = ROWS - TAIL

PIECE = ROWS + REST

NOTES = 16
FAR_NOTES = 8
FIELD = 2**16
PARTS = 8
TOP = 32767.0
DIGIT = 4096.0
MIDDLE = 32768.0
MARGIN = 0.01
FINE = 8.0


def lane_group(shape):
    return lax.broadcasted_iota(jnp.int32, shape, 1) // STEP


def rolled(v, by):
    return pltpu.roll(v, by % LANES, 1)


def folded(res, k):
    free = QUAD - 1 - k
    tail = res[REST:]
    group = lane_group((TAIL, LANES))
    return jnp.concatenate(
        [jnp.where(group == free, rolled(tail, STEP * (m + 1)), res[m * TAIL : (m + 1) * TAIL]) for m in range(QUAD - 1)],
        axis=0,
    )


def unfolded(piece, k):
    free = QUAD - 1 - k
    group = lane_group((TAIL, LANES))
    tail = rolled(piece[:TAIL], -STEP)
    for m in range(1, QUAD - 1):
        moved = rolled(piece[m * TAIL : (m + 1) * TAIL], -STEP * (m + 1))
        tail = jnp.where(group == (free - m - 1) % QUAD, moved, tail)
    return jnp.concatenate([piece, tail], axis=0)


def own_parts(block, k):
    at = STEP * k
    res = [block[:, at + LANES :], jnp.zeros((ROWS, STEP), block.dtype), block[:, :at]]
    return block[:, at : at + LANES], folded(jnp.concatenate([r for r in res if r.shape[1]], axis=1), k)


def own_block(tile, piece, k):
    at = STEP * k
    res = unfolded(piece, k)
    parts = [res[:, LANES - at :] if k else res[:, :0], tile, res[:, : LANES - STEP - at]]
    return jnp.concatenate([p for p in parts if p.shape[1]], axis=1)


def own_place():
    return lax.axis_index("zl") * 2 + lax.axis_index("c")


def for_core(first, second):
    core = lax.axis_index("c")
    pl.when(core == 0)(first)
    pl.when(core != 0)(second)


def in_rows(values, rows):
    row = lax.broadcasted_iota(jnp.int32, (rows, LANES), 0)
    out = jnp.zeros((rows, LANES), F32)
    for i, value in enumerate(values):
        out = jnp.where(row == i, value, out)
    return out


def digits(value):
    whole = jnp.floor(value)
    part = (value - whole) * DIGIT
    digit = jnp.floor(part)
    return whole, digit, jnp.floor((part - digit) * DIGIT)


def from_digits(whole, first, second):
    return whole + (first + second * (1 / DIGIT)) * (1 / DIGIT)


def coded(total):
    largest = jnp.maximum(jnp.max(jnp.abs(total), axis=0, keepdims=True), 1e-30)
    level = jnp.ceil(FINE * jnp.log2(largest) + MARGIN)
    units = jnp.round(total * (TOP * jnp.exp2(level * (-1 / FINE))))
    return short(units), level


def short(values):
    return values.astype(jnp.int32).astype(jnp.int16)


def wide(values):
    return values.astype(jnp.int32).astype(F32)


def decoded(units, level):
    return (jnp.exp2(level * (1 / FINE)) * (1 / TOP)) * wide(units)


def fields(both):
    return both // FIELD, both % FIELD


def own_pieces(fast, g, core):
    group = lane_group((ROWS, LANES))
    lanes = [slice(g * WIDE + i * LANES, g * WIDE + (i + 1) * LANES) for i in range(2 * QUAD - 1)]
    odd = [fast[:, at].astype(F32) for at in lanes[1::2]]
    pieces = []
    for k in range(core, QUAD, 2):
        if k == 0:
            res = odd[0]
        elif k == QUAD - 1:
            res = odd[-1]
        else:
            res = jnp.where(group >= QUAD - k, odd[k - 1], odd[k])
        pieces.append((fast[:, lanes[2 * k]].astype(F32), folded(res, k)))
    return pieces


def for_own_place(body):
    place = own_place()
    for k in range(QUAD):
        pl.when(place == k)(lambda k=k: body(k))


def sort_kernel(fast, slow, keep, mine):
    nx, n_zl, n_zh = keep.shape[:3]

    def pack(k):
        mine[:ROWS], mine[ROWS:] = own_parts(slow[0, 0], k)

    for_own_place(pack)

    def body(core):
        for g in range(nx * n_zh):
            x, zh = divmod(g, n_zh)
            for zl, (tile, rest) in enumerate(own_pieces(fast, g, core)):
                keep[x, zl, zh, :ROWS] = tile.astype(BF16)
                keep[x, zl, zh, ROWS:] = rest.astype(BF16)

    for_core(lambda: body(0), lambda: body(1))


def pair_sum_kernel(counts, keep, other, out):
    nx, n_zl, n_zh = keep.shape[:3]

    def body(core):
        pair = lax.axis_index("expert") * 2
        both = [counts[pair + c, 0] for c in (core, 1 - core)]
        tokens, steps = ([jnp.full((1, LANES), v.astype(F32)) for v in f] for f in zip(*map(fields, both)))
        shares = [t / n for t, n in zip(tokens, steps)]
        everywhere = sum(fields(counts[i, 0])[0] for i in range(counts.shape[0])).astype(F32)
        work = sum(t * n for t, n in zip(tokens, steps))
        sums = (sum(tokens), work, *digits(sum(shares)), everywhere)
        levels = [[] for _ in range(out.shape[0])]
        for g in range(nx * n_zh):
            x, zh = divmod(g, n_zh)
            for zl, parts in enumerate(own_pieces(other, g, core)):
                d = x * n_zl + zl
                mix = shares[0] * keep[x, zl, zh].astype(F32) + shares[1] * jnp.concatenate(parts, axis=0)
                out[d, zh * PIECE : (zh + 1) * PIECE], level = coded(mix)
                levels[d].append(level)
        for d in range(out.shape[0]):
            out[d, n_zh * PIECE :] = short(in_rows((*levels[d], *sums), NOTES))

    for_core(lambda: body(0), lambda: body(1))


def near_sum_kernel(got, out):
    n, n_zh = got.shape[0], out.shape[0]
    notes = [wide(got[s, n_zh * PIECE :]) for s in range(n)]
    tok, work, *qsum, everywhere = (sum(v[n_zh + i : n_zh + i + 1] for v in notes) for i in range(6))
    high = jnp.floor(work / DIGIT)
    far = (tok, high, work - DIGIT * high, everywhere - MIDDLE, *digits(from_digits(*qsum)))
    for zh in range(n_zh):
        piece = slice(zh * PIECE, (zh + 1) * PIECE)
        total = decoded(got[0, piece], notes[0][zh : zh + 1])
        for s in range(1, n):
            total = total + decoded(got[s, piece], notes[s][zh : zh + 1])
        out[zh, :PIECE], level = coded(total)
        out[zh, PIECE:] = short(in_rows((level, *far), FAR_NOTES))


def refresh_kernel(groups, got, mine, fresh, copies):
    total = sums = None
    for s in range(got.shape[0]):
        notes = wide(got[s, PIECE:])
        part = decoded(got[s, :PIECE], notes[0:1])
        total, sums = (part, notes) if s == 0 else (total + part, sums + notes)
    tok = sums[1:2]
    work = DIGIT * sums[2:3] + sums[3:4]
    everywhere = sums[4:5] + MIDDLE * got.shape[0]
    qsum = from_digits(sums[5:6], sums[6:7], sums[7:8])
    rate = outer_rate * groups * work / (tok * everywhere)
    new = mine[...] + rate * (total - qsum * mine[...])
    fresh[...] = new
    for i in range(copies.shape[0]):
        copies[i] = new.astype(BF16)


def side_kernel(fresh, own, new_slow, half):
    def unpack(k):
        new_slow[0, 0] = own_block(fresh[:ROWS], fresh[ROWS:], k)

    for_own_place(unpack)

    def body(core):
        for at, k, piece in pieces_of(own, core):
            half[:, at + 2 * k * LANES : at + (2 * k + 1) * LANES] = piece[:ROWS]
            res = unfolded(piece[ROWS:].astype(F32), k).astype(BF16)
            for i in beside(k):
                half[:, at + i * LANES : at + (i + 1) * LANES] = res

    for_core(lambda: body(0), lambda: body(1))


def pieces_of(pieces, core):
    for g in range(pieces.shape[0] * pieces.shape[2]):
        x, zh = divmod(g, pieces.shape[2])
        for zl in range(pieces.shape[1]):
            yield g * WIDE, 2 * zl + core, pieces[x, zl, zh]


def beside(k):
    return [i for i in (2 * k - 1, 2 * k + 1) if 0 < i < 2 * QUAD - 1]


def lay_out_kernel(half, other, out, whole, sems):
    part = whole.shape[1] // sems.shape[0]
    group = lane_group((ROWS, LANES))

    def body(core):
        stores = []
        for at, k, piece in pieces_of(other, 1 - core):
            mine = at + 2 * (k + 2 * core - 1) * LANES
            whole[:, mine : mine + LANES] = half[:, mine : mine + LANES]
            whole[:, at + 2 * k * LANES : at + (2 * k + 1) * LANES] = piece[:ROWS]
            res = unfolded(piece[ROWS:].astype(F32), k)
            for i in beside(k):
                span = slice(at + i * LANES, at + (i + 1) * LANES)
                left = group < QUAD - 1 - i // 2
                theirs = left if i > 2 * k else jnp.logical_not(left)
                whole[:, span] = jnp.where(theirs, res, half[:, span].astype(F32)).astype(BF16)
            if k // 2 == 1 and (at + WIDE) % part == 0:
                i = at // part
                span = pl.ds(i * part, part)
                stores.append(pltpu.make_async_copy(whole.at[:, span], out.at[:, span], sems.at[i]))
                stores[-1].start()
        for store in stores:
            store.wait()

    for_core(lambda: body(0), lambda: body(1))


def call(kernel, out_shape, **more):
    return pl.pallas_call(
        kernel,
        out_shape=out_shape,
        compiler_params=pltpu.CompilerParams(vmem_limit_bytes=48 * 2**20),
        **more,
    )


def struct(shape, dtype):
    return jax.ShapeDtypeStruct(shape, dtype)


def swap(pieces, axis):
    return lax.all_to_all(pieces, axis, split_axis=0, concat_axis=0, tiled=True)


SCALAR = pl.BlockSpec(memory_space=pltpu.SMEM)
WHOLE = pl.BlockSpec(memory_space=pltpu.VMEM)


def shards(fast_weights, slow_weights, step_counts, token_counts):
    size = {a: lax.axis_size(a) for a in SHARD}
    groups = lax.axis_size("expert")
    nx, nzh = size["x"], size["zh"]
    fast = fast_weights[0, 0, 0]

    plane = nx * size["zl"]
    both = token_counts * FIELD + step_counts
    counts = swap(jnp.broadcast_to(both, (groups * size["c"], 1)), ("expert", "c"))
    other = lax.ppermute(fast, "c", [(0, 1), (1, 0)])
    shape = (nx, size["zl"], nzh, PIECE, LANES)
    block = struct((PIECE, LANES), F32)
    keep, mine = call(sort_kernel, (struct(shape, BF16), block))(fast, slow_weights)
    pairs = call(
        pair_sum_kernel,
        struct((plane, nzh * PIECE + NOTES, LANES), jnp.int16),
        in_specs=[SCALAR, WHOLE, WHOLE],
    )(counts, keep, other)
    got = swap(pairs, ("x", "zl"))
    sums = call(near_sum_kernel, struct((nzh, PIECE + FAR_NOTES, LANES), jnp.int16))(got)
    got = swap(sums, "zh")
    fresh, copies = call(
        lambda *refs: refresh_kernel(groups, *refs), (block, struct((nzh, PIECE, LANES), BF16))
    )(got, mine)

    column = swap(copies, "zh")
    own = swap(jnp.broadcast_to(column[None], (plane, *column.shape)), ("x", "zl"))
    other = lax.ppermute(own, "c", [(0, 1), (1, 0)])
    new_slow, half = call(side_kernel, (struct(slow_weights.shape, F32), struct(fast.shape, BF16)))(
        fresh, own.reshape(shape)
    )
    reset = call(
        lay_out_kernel,
        struct(fast.shape, BF16),
        out_specs=pl.BlockSpec(memory_space=pltpu.HBM),
        scratch_shapes=[pltpu.VMEM(fast.shape, BF16), pltpu.SemaphoreType.DMA((PARTS,))],
    )(half, other.reshape(shape))
    return new_slow, reset[None, None]


def solution(mesh):
    torus = Mesh(
        mesh.devices.reshape(mesh.shape["expert"], 2, 8, 2, 2),
        ("expert", *SHARD),
    )
    placed = (
        P("expert", SHARD, None, None, None),
        P("expert", None, None, SHARD),
        P("expert", SHARD),
        P("expert", SHARD),
    )
    return jax.shard_map(
        shards,
        mesh=torus,
        in_specs=placed,
        out_specs=(P("expert", None, None, SHARD), P("expert", None, None, None)),
        check_vma=False,
    )
```
